256 devices in a mesh: term: 32 (over z_lo, y, core), wave: 8 (over x, z_hi).
Axes of the slice: x: 4, y: 4, z: 8 (z_hi: 2, z_lo: 4; z = z_hi * 4 + z_lo), core: 2. Of those that a mesh axis runs over, the one named last changes fastest.
Arguments:
- spectral_state: bfloat16 [32, 512, 1280], P('wave', 'term'), may hold values from -6 to 6
- inverse: bfloat16 [32, 32, 2, 640, 640], P('term', 'wave'), may hold values from -0.15625 to 0.15625
- term_weights: float32 [32, 2], P('term'), may hold values from -2.5 to 2.5
- legendre: bfloat16 [32, 640, 1280], P('wave'), may hold values from -0.25 to 0.25
- slot_column: int32 [32], replicated, may hold values from 0 to 31, each once
Outputs:
- fourier: float32 [32, 2, 512, 1280], P(None, None, 'term', 'wave')
The draws below stay inside these ranges and needn't reach their ends.
Inputs may be any that keep to these rules, and one draw needn't show every extreme that they name: `slot_column`: each column appears in exactly one slot.
All inputs are finite; a program needn't handle non-finite values.
Results may differ from the reference program's by a relative error of at most 0.0003.
Values may be sent and summed in bfloat16 or wider, within the bound.
A program may use at most 128 MiB of HBM per device.

```python
import jax
import jax.numpy as jnp
from jax import lax

NDEG = 640
NLAT = 1280
COLS = 512
M_TOT = 32
TERMS = 32


def block_scale(own_key, dims, shards, least, top_value):
    def one(axis_at, shards_of):
        heights = jax.random.uniform(jax.random.fold_in(jax.random.fold_in(own_key, 6), axis_at), (shards_of,), jnp.float32, least / len(shards), top_value / len(shards))
        return jnp.repeat(jnp.exp(heights), dims[axis_at] // shards_of).reshape((-1,) + (1,) * (len(dims) - axis_at - 1))

    level = one(*shards[0])
    for cut in shards[1:]:
        level = level * one(*cut)
    return level


def bell_draw(own_key, shape, deviation, limit, cuts=(), kind=jnp.bfloat16):
    values = deviation * jax.random.normal(own_key, shape, jnp.float32)
    if cuts:
        values = values * block_scale(own_key, shape, cuts, -0.22, 0.18)
    return jnp.clip(values, -limit, limit).astype(kind)


def setup_inputs(seed: int = 0) -> dict:
    streams_of = jax.random.split(jax.random.key(seed), 6)
    spectral_state = bell_draw(streams_of[0], (M_TOT, COLS, 2 * NDEG), 1.0, 6.0, ((0, 8), (1, 32)))
    inverse = bell_draw(streams_of[1], (TERMS, M_TOT, 2, NDEG, NDEG), (2 * NDEG) ** -0.5, 0.15625, ((0, 32), (1, 8)))
    term_weights = bell_draw(streams_of[2], (TERMS, 2), (TERMS ** -0.5), 2.5, ((0, 32),), jnp.float32)
    legendre = bell_draw(streams_of[3], (M_TOT, NDEG, NLAT), NDEG ** -0.5, 0.25, ((0, 8),))
    slot_column = jax.random.permutation(streams_of[4], M_TOT).astype(jnp.int32)
    return {"spectral_state": spectral_state, "inverse": inverse, "term_weights": term_weights, "legendre": legendre, "slot_column": slot_column}


def reference(spectral_state, inverse, term_weights, legendre, slot_column):
    highest = lax.Precision.HIGHEST

    def one_slot(slot_index):
        values = lax.dynamic_index_in_dim(spectral_state, slot_index, 0, keepdims=False)
        blocks = lax.dynamic_index_in_dim(inverse, slot_index, 1, keepdims=False)
        table = lax.dynamic_index_in_dim(legendre, slot_index, 0, keepdims=False)
        middle = values.shape[1] // 2
        real_in = values[:, :middle].astype(jnp.float32)
        imag_in = values[:, middle:].astype(jnp.float32)
        real_block = blocks[:, 0].astype(jnp.float32)
        imag_block = blocks[:, 1].astype(jnp.float32)
        real_real = jnp.einsum("cn,kno->kco", real_in, real_block, precision=highest)
        imag_imag = jnp.einsum("cn,kno->kco", imag_in, imag_block, precision=highest)
        real_imag = jnp.einsum("cn,kno->kco", real_in, imag_block, precision=highest)
        imag_real = jnp.einsum("cn,kno->kco", imag_in, real_block, precision=highest)
        solved_re = real_real - imag_imag
        solved_im = real_imag + imag_real
        weight_re = term_weights[:, 0][:, None, None]
        weight_im = term_weights[:, 1][:, None, None]
        total_re = jnp.sum(weight_re * solved_re - weight_im * solved_im, axis=0)
        total_im = jnp.sum(weight_re * solved_im + weight_im * solved_re, axis=0)
        total = jnp.stack([total_re, total_im], axis=0)
        return jnp.einsum("pcn,nl->pcl", total, table.astype(jnp.float32), precision=highest)

    slot_count = spectral_state.shape[0]
    grids = lax.map(one_slot, jnp.arange(slot_count, dtype=jnp.int32))
    fourier = jnp.zeros(grids.shape, jnp.float32).at[slot_column].set(grids)
    return fourier
```

```python
import functools

import jax
import jax.numpy as jnp
from jax import lax
from jax.experimental import pallas as pl
from jax.experimental.pallas import tpu as pltpu
from jax.sharding import PartitionSpec as P

F32 = jnp.float32
BF16 = jnp.bfloat16
I32 = jnp.int32
MESH = pl.DeviceIdType.MESH

NY, NZ, NC, NW = 4, 4, 2, 8
NDEG, NLAT = 640, 1280
OWN = 16
HALF = NDEG // NC
QUARTER = HALF // 2
LANES = 128
TILES = NDEG // LANES
MSG = QUARTER + 8
WINDOW = 384
STEPS = 8.0
TOP = 32700.0
BAND = NLAT // NW
ROWS = NY * OWN
CHUNK = 32


def code_of(height):
    return jnp.ceil(jnp.log2(jnp.maximum(height, 1e-30)) * STEPS).astype(I32)


def span_of(code):
    return jnp.exp2(code.astype(F32) * (1.0 / STEPS))


def gain_of(code):
    return TOP * jnp.exp2(code.astype(F32) * (-1.0 / STEPS))


def packed(real, imag, gain):
    high = (real * gain + 32768.5).astype(I32)
    low = (imag * gain + 32768.5).astype(I32)
    return lax.shift_left(high, jnp.full_like(high, 16)) | low


def unpacked(code, step):
    high = lax.shift_right_logical(code, jnp.full_like(code, 16)).astype(F32)
    low = (code & 0xFFFF).astype(F32)
    return (high - 32768.0) * step, (low - 32768.0) * step


def exchange_kernel(
    x_hbm, inv_hbm, w_ref, leg_hbm, out_ref,
    raw_own, raw_pal, w_pal, x_all, leg, snd, rcv, work, rhs_a, rhs_b,
    t_own, t_snd, t_rcv, z_snd, z_rcv, t_fin, grid, pieces,
    raw_own_sem, raw_pal_sem, w_sem, x_snd_sem, x_rcv_sem, x_fwd_sem, leg_sem,
    snd_sem, rcv_sem, t_snd_sem, t_rcv_sem, z_snd_sem, z_rcv_sem, f_snd_sem, f_rcv_sem,
):
    term = lax.axis_index("term")
    wave = lax.axis_index("wave")
    core = lax.rem(term, 2)
    y = lax.rem(term // 2, NY)
    z = term // (2 * NY)
    zy = z * NY + y

    def at(z_, y_, core_, wave_):
        return ((z_ * NY + y_) * 2 + core_, wave_)

    pal = at(z, y, 1 - core, wave)

    def own_copy(j):
        return pltpu.make_async_copy(
            inv_hbm.at[0, :, :, pl.ds(pl.multiple_of(core * HALF, 64), HALF), pl.ds(pl.multiple_of(j * LANES, LANES), LANES)],
            raw_own.at[j],
            raw_own_sem.at[j],
        )

    def pal_copy(j):
        return pltpu.make_async_remote_copy(
            src_ref=inv_hbm.at[0, :, :, pl.ds(pl.multiple_of((1 - core) * HALF, 64), HALF), pl.ds(pl.multiple_of(j * LANES, LANES), LANES)],
            dst_ref=raw_pal.at[j],
            send_sem=raw_pal_sem.at[0, j],
            recv_sem=raw_pal_sem.at[1, j],
            device_id=pal,
            device_id_type=MESH,
        )

    w_copy = pltpu.make_async_remote_copy(
        src_ref=w_ref, dst_ref=w_pal, send_sem=w_sem.at[0], recv_sem=w_sem.at[1], device_id=pal, device_id_type=MESH
    )

    def x_row():
        return pl.ds(pl.multiple_of(zy * OWN, OWN), OWN)

    def x_copy(i):
        peer = lax.rem(zy + i, NZ * NY)
        return pltpu.make_async_remote_copy(
            src_ref=x_hbm.at[lax.rem(peer, NY)],
            dst_ref=x_all.at[core, x_row()],
            send_sem=x_snd_sem.at[i],
            recv_sem=x_rcv_sem.at[i],
            device_id=at(peer // NY, lax.rem(peer, NY), core, wave),
            device_id_type=MESH,
        )

    x_local = pltpu.make_async_copy(x_hbm.at[y], x_all.at[core, x_row()], x_rcv_sem.at[0])
    x_forward = pltpu.make_async_remote_copy(
        src_ref=x_all.at[core],
        dst_ref=x_all.at[core],
        send_sem=x_fwd_sem.at[0],
        recv_sem=x_fwd_sem.at[1],
        device_id=pal,
        device_id_type=MESH,
    )
    leg_copy = pltpu.make_async_copy(leg_hbm.at[y], leg, leg_sem)

    def y_copy(kind, way, j):
        to = lax.rem(y + (1 if way == 0 else NY - 1), NY)
        return pltpu.make_async_remote_copy(
            src_ref=snd.at[kind, way, j],
            dst_ref=rcv.at[kind, way, j],
            send_sem=snd_sem.at[kind, way, j],
            recv_sem=rcv_sem.at[kind, way, j],
            device_id=at(z, to, core, wave),
            device_id_type=MESH,
        )

    def t_copy(j):
        return pltpu.make_async_remote_copy(
            src_ref=t_snd.at[j],
            dst_ref=t_rcv.at[j],
            send_sem=t_snd_sem.at[j],
            recv_sem=t_rcv_sem.at[j],
            device_id=pal,
            device_id_type=MESH,
        )

    def z_copy(i, j):
        return pltpu.make_async_remote_copy(
            src_ref=z_snd.at[i, j],
            dst_ref=z_rcv.at[i, j],
            send_sem=z_snd_sem.at[i, j],
            recv_sem=z_rcv_sem.at[i, j],
            device_id=at(lax.rem(z + 1 + i, NZ), y, core, wave),
            device_id_type=MESH,
        )

    def f_copy(dy, dw):
        to_y = lax.rem(y + dy, NY)
        to_w = lax.rem(wave + dw, NW)
        return pltpu.make_async_remote_copy(
            src_ref=pieces.at[to_y, to_w],
            dst_ref=out_ref.at[y, wave],
            send_sem=f_snd_sem.at[dy, dw],
            recv_sem=f_rcv_sem.at[dy, dw],
            device_id=at(z, to_y, core, to_w),
            device_id_type=MESH,
        )

    def f_arrival(dy, dw):
        from_y = lax.rem(y + NY - dy, NY)
        from_w = lax.rem(wave + NW - dw, NW)
        return pltpu.make_async_remote_copy(
            src_ref=pieces.at[from_y, from_w],
            dst_ref=out_ref.at[from_y, from_w],
            send_sem=f_snd_sem.at[dy, dw],
            recv_sem=f_rcv_sem.at[dy, dw],
            device_id=at(z, from_y, core, from_w),
            device_id_type=MESH,
        )

    def x_arrival(i):
        peer = lax.rem(zy + NZ * NY - i, NZ * NY)
        return pltpu.make_async_remote_copy(
            src_ref=x_hbm.at[y],
            dst_ref=x_all.at[core, pl.ds(pl.multiple_of(peer * OWN, OWN), OWN)],
            send_sem=x_snd_sem.at[i],
            recv_sem=x_rcv_sem.at[i],
            device_id=at(peer // NY, lax.rem(peer, NY), core, wave),
            device_id_type=MESH,
        )

    x_forward_arrival = pltpu.make_async_remote_copy(
        src_ref=x_all.at[1 - core],
        dst_ref=x_all.at[1 - core],
        send_sem=x_fwd_sem.at[0],
        recv_sem=x_fwd_sem.at[1],
        device_id=pal,
        device_id_type=MESH,
    )

    barrier = pltpu.get_barrier_semaphore()
    pl.semaphore_signal(barrier, inc=1, device_id=pal, device_id_type=MESH)

    @pl.loop(1, NZ * NY)
    def _(i):
        peer = lax.rem(zy + i, NZ * NY)
        pl.semaphore_signal(
            barrier, inc=1, device_id=at(peer // NY, lax.rem(peer, NY), core, wave), device_id_type=MESH
        )

    @pl.loop(0, NY * (NW - 1))
    def _(i):
        pl.semaphore_signal(
            barrier,
            inc=1,
            device_id=at(z, i // (NW - 1), core, lax.rem(wave + 1 + lax.rem(i, NW - 1), NW)),
            device_id_type=MESH,
        )

    @pl.loop(0, TILES)
    def _(j):
        own_copy(j).start()

    x_local.start()
    leg_copy.start()
    pad = pl.ds(pl.multiple_of((1 - core) * HALF, 64), WINDOW - HALF)
    for side in range(2):
        rhs_a[side, pad, :] = jnp.zeros((WINDOW - HALF, 2 * LANES), BF16)
        rhs_b[side, pad, :] = jnp.zeros((WINDOW - HALF, 2 * LANES), BF16)
    grid[...] = jnp.zeros_like(grid)

    pl.semaphore_wait(barrier, 1 + (NZ * NY - 1) + NY * (NW - 1))

    w_copy.start()

    @pl.loop(0, TILES)
    def _(j):
        pal_copy(j).start()

    @pl.loop(1, NZ * NY)
    def _(i):
        x_copy(i).start()

    w_copy.wait()
    weights = [w_ref[0:1, 0:1], w_ref[0:1, 1:2], w_pal[0:1, 0:1], w_pal[0:1, 1:2]]
    weights = [jnp.broadcast_to(v, (CHUNK, LANES)) for v in weights]

    def term_sum(j, slot, row):
        rows = pl.ds(row, CHUNK)
        r0 = raw_own[j, slot, 0, rows, :].astype(F32)
        j0 = raw_own[j, slot, 1, rows, :].astype(F32)
        r1 = raw_pal[j, slot, 0, rows, :].astype(F32)
        j1 = raw_pal[j, slot, 1, rows, :].astype(F32)
        a0, b0, a1, b1 = weights
        return (a0 * r0 - b0 * j0) + (a1 * r1 - b1 * j1), (a0 * j0 + b0 * r0) + (a1 * j1 + b1 * r1)

    def higher(height, real, imag):
        tall = jnp.maximum(jnp.abs(real), jnp.abs(imag))
        return jnp.maximum(height, jnp.max(tall.reshape(-1, 8, LANES), axis=0))

    def write_message(to, j, slot, half, since):
        height = jnp.zeros((8, LANES), F32)
        if since is not None:
            step = span_of(since[QUARTER : QUARTER + 8, :])[0:1] * (1.0 / TOP)
            step = jnp.broadcast_to(step, (CHUNK, LANES))
        for part in range(QUARTER // CHUNK):
            rows = slice(part * CHUNK, (part + 1) * CHUNK)
            real, imag = term_sum(j, slot, half * QUARTER + part * CHUNK)
            if since is not None:
                more_real, more_imag = unpacked(since[rows, :], step)
                real, imag = real + more_real, imag + more_imag
            work[0, rows, :] = real
            work[1, rows, :] = imag
            height = higher(height, real, imag)
        height = jnp.broadcast_to(jnp.max(height, axis=0, keepdims=True), (8, LANES))
        code = code_of(height)
        gain = jnp.broadcast_to(gain_of(code)[0:1], (CHUNK, LANES))
        for part in range(QUARTER // CHUNK):
            rows = slice(part * CHUNK, (part + 1) * CHUNK)
            to[rows, :] = packed(work[0, rows, :], work[1, rows, :], gain)
        to[QUARTER : QUARTER + 8, :] = code

    def stage_first(j):
        own_copy(j).wait()
        pal_copy(j).wait_recv()
        for way in range(2):
            write_message(snd.at[0, way, j], j, lax.rem(y + 2, NY), way, None)
            y_copy(0, way, j).start()
        for way in range(2):
            slot = lax.rem(y + (1 if way == 0 else NY - 1), NY)
            write_message(snd.at[1, way, j], j, slot, 1 - way, None)
            y_copy(1, way, j).start()

    def stage_sum(j):
        for way in range(2):
            slot = lax.rem(y + (1 if way == 0 else NY - 1), NY)
            y_copy(0, way, j).wait_recv()
            write_message(snd.at[2, way, j], j, slot, way, rcv.at[0, way, j])
            y_copy(2, way, j).start()

    def stage_product(j):
        for kind in (1, 2):
            for way in range(2):
                y_copy(kind, way, j).wait_recv()
        for half in range(2):
            first = rcv.at[2, half, j]
            second = rcv.at[1, 1 - half, j]
            steps = [
                jnp.broadcast_to(span_of(part[QUARTER : QUARTER + 8, :])[0:1] * (1.0 / TOP), (CHUNK, LANES))
                for part in (first, second)
            ]
            for part in range(QUARTER // CHUNK):
                rows = slice(part * CHUNK, (part + 1) * CHUNK)
                start = half * QUARTER + part * CHUNK
                real, imag = term_sum(j, y, start)
                for source, step in zip((first, second), steps):
                    more_real, more_imag = unpacked(source[rows, :], step)
                    real, imag = real + more_real, imag + more_imag
                real_high = real.astype(BF16)
                imag_high = imag.astype(BF16)
                real_low = (real - real_high.astype(F32)).astype(BF16)
                imag_low = (imag - imag_high.astype(F32)).astype(BF16)
                into = pl.ds(pl.multiple_of(core * (WINDOW - HALF) + start, CHUNK), CHUNK)
                rhs_a[0, into, :] = jnp.concatenate([real_high, imag_high], axis=1)
                rhs_a[1, into, :] = jnp.concatenate([real_low, imag_low], axis=1)
                rhs_b[0, into, :] = jnp.concatenate([-imag_high, real_high], axis=1)
                rhs_b[1, into, :] = jnp.concatenate([-imag_low, real_low], axis=1)

        def product(owner, row):
            rows = pl.ds(pl.multiple_of(row, 128), 128)
            left = x_all[owner, rows, pl.ds(pl.multiple_of(core * 256, LANES), WINDOW)]
            right = x_all[owner, rows, pl.ds(pl.multiple_of(NDEG + core * 256, LANES), WINDOW)]
            value = jnp.dot(left, rhs_a[0], preferred_element_type=F32)
            value += jnp.dot(right, rhs_b[0], preferred_element_type=F32)
            value += jnp.dot(left, rhs_a[1], preferred_element_type=F32)
            value += jnp.dot(right, rhs_b[1], preferred_element_type=F32)
            return value

        @pl.loop(0, 2)
        def _(i):
            t_snd[j, pl.ds(pl.multiple_of(i * 128, 128), 128), :] = product(1 - core, i * 128)

        t_copy(j).start()

        @pl.loop(0, 2)
        def _(i):
            t_own[j, pl.ds(pl.multiple_of(i * 128, 128), 128), :] = product(core, i * 128)

    def stage_spread(j):
        t_copy(j).wait_recv()
        for i in range(NZ):
            to = lax.rem(z + 1 + i, NZ)
            rows = pl.ds(pl.multiple_of(to * ROWS, ROWS), ROWS)
            value = t_own[j, rows, :] + t_rcv[j, rows, :]
            if i == NZ - 1:
                t_fin[j] = value
                continue
            real, imag = value[:, :LANES], value[:, LANES:]
            height = higher(jnp.zeros((8, LANES), F32), real, imag)
            height = jnp.broadcast_to(jnp.max(height, axis=0, keepdims=True), (8, LANES))
            code = code_of(height)
            gain = jnp.broadcast_to(gain_of(code)[0:1], (ROWS, LANES))
            z_snd[i, j, :ROWS, :] = packed(real, imag, gain)
            z_snd[i, j, ROWS:, :] = code
            z_copy(i, j).start()

    def stage_synthesis(j):
        value = t_fin[j]
        real, imag = value[:, :LANES], value[:, LANES:]
        for i in range(NZ - 1):
            z_copy(i, j).wait_recv()
            step = span_of(z_rcv[i, j, ROWS:, :])[0:1] * (1.0 / TOP)
            step = jnp.broadcast_to(step, (ROWS, LANES))
            more_real, more_imag = unpacked(z_rcv[i, j, :ROWS, :], step)
            real, imag = real + more_real, imag + more_imag
        both = jnp.concatenate([real, imag], axis=0)
        high = both.astype(BF16)
        low = (both - high.astype(F32)).astype(BF16)
        left = jnp.concatenate([high, low], axis=0)
        table = pl.ds(pl.multiple_of(j * LANES, LANES), LANES)

        @pl.loop(0, NLAT // 256)
        def _(i):
            columns = pl.ds(pl.multiple_of(i * 256, 256), 256)
            value = jnp.dot(left, leg[table, columns], preferred_element_type=F32)
            grid[:, columns] += value[: 2 * ROWS] + value[2 * ROWS :]

    @pl.loop(0, TILES + 4)
    def _(it):
        @pl.when(it < TILES)
        def _():
            stage_first(it)

        @pl.when((it >= 1) & (it < TILES + 1))
        def _():
            stage_sum(it - 1)

        @pl.when(it == 2)
        def _():
            x_local.wait()

            @pl.loop(1, NZ * NY)
            def _(i):
                x_arrival(i).wait_recv()

            x_forward.start()
            x_forward_arrival.wait_recv()

        @pl.when((it >= 2) & (it < TILES + 2))
        def _():
            stage_product(it - 2)

        @pl.when((it >= 3) & (it < TILES + 3))
        def _():
            stage_spread(it - 3)

        @pl.when(it == 4)
        def _():
            leg_copy.wait()

        @pl.when(it >= 4)
        def _():
            stage_synthesis(it - 4)

    lane = lax.broadcasted_iota(I32, (8, LANES), 1)
    for to_y in range(NY):
        rows = slice(to_y * OWN, (to_y + 1) * OWN)
        real = grid[rows, :]
        imag = grid[ROWS + to_y * OWN : ROWS + (to_y + 1) * OWN, :]
        height = jnp.max(jnp.maximum(jnp.abs(real), jnp.abs(imag)), axis=1, keepdims=True)
        code = code_of(jnp.broadcast_to(height, (OWN, LANES)))
        gain = gain_of(code)
        gain = jnp.concatenate([gain] * (NLAT // LANES), axis=1)
        value = packed(real, imag, gain)
        for to_w in range(NW):
            tile, skip = divmod(to_w * BAND, LANES)
            band = value[:, tile * LANES : tile * LANES + 2 * LANES]
            if skip:
                band = pltpu.roll(band, 2 * LANES - skip, 1)
            rest = band[:, LANES:]
            last = jnp.where(lane < 96, code[:8], code[8:])
            last = jnp.where(lane < 64, pltpu.roll(rest[8:], 32, 1), last)
            last = jnp.where(lane < 32, rest[:8], last)
            pieces[to_y, to_w, :OWN, :] = band[:, :LANES]
            pieces[to_y, to_w, OWN:, :] = last

    @pl.loop(1, NW)
    def _(dw):
        @pl.loop(0, NY)
        def _(dy):
            f_copy(dy, dw).start()

    @pl.loop(1, NY)
    def _(dy):
        f_copy(dy, 0).start()

    out_ref[y, wave] = pieces[y, wave]

    @pl.loop(0, TILES)
    def _(j):
        pal_copy(j).wait_send()
        t_copy(j).wait_send()
        for kind in range(3):
            for way in range(2):
                y_copy(kind, way, j).wait_send()
        for i in range(NZ - 1):
            z_copy(i, j).wait_send()

    @pl.loop(1, NZ * NY)
    def _(i):
        x_copy(i).wait_send()

    x_forward.wait_send()

    @pl.loop(1, NW)
    def _(dw):
        @pl.loop(0, NY)
        def _(dy):
            f_arrival(dy, dw).wait_recv()
            f_copy(dy, dw).wait_send()

    @pl.loop(1, NY)
    def _(dy):
        f_arrival(dy, 0).wait_recv()
        f_copy(dy, 0).wait_send()


def exchange(spectral_state, inverse, term_weights, legendre):
    any_space = pl.BlockSpec(memory_space=pl.ANY)
    vmem = pl.BlockSpec(memory_space=pltpu.VMEM)
    dma = pltpu.SemaphoreType.DMA
    return pl.pallas_call(
        exchange_kernel,
        out_shape=jax.ShapeDtypeStruct((NY, NW, OWN + 8, LANES), I32),
        in_specs=[any_space, any_space, vmem, any_space],
        out_specs=vmem,
        scratch_shapes=[
            pltpu.VMEM((TILES, NY, 2, HALF, LANES), BF16),
            pltpu.VMEM((TILES, NY, 2, HALF, LANES), BF16),
            pltpu.VMEM((1, 2), F32),
            pltpu.VMEM((2, NZ * NY * OWN, 2 * NDEG), BF16),
            pltpu.VMEM((NDEG, NLAT), BF16),
            pltpu.VMEM((3, 2, TILES, MSG, LANES), I32),
            pltpu.VMEM((3, 2, TILES, MSG, LANES), I32),
            pltpu.VMEM((2, QUARTER, LANES), F32),
            pltpu.VMEM((2, WINDOW, 2 * LANES), BF16),
            pltpu.VMEM((2, WINDOW, 2 * LANES), BF16),
            pltpu.VMEM((TILES, 256, 2 * LANES), F32),
            pltpu.VMEM((TILES, 256, 2 * LANES), F32),
            pltpu.VMEM((TILES, 256, 2 * LANES), F32),
            pltpu.VMEM((NZ - 1, TILES, ROWS + 8, LANES), I32),
            pltpu.VMEM((NZ - 1, TILES, ROWS + 8, LANES), I32),
            pltpu.VMEM((TILES, ROWS, 2 * LANES), F32),
            pltpu.VMEM((2 * ROWS, NLAT), F32),
            pltpu.VMEM((NY, NW, OWN + 8, LANES), I32),
            dma((TILES,)),
            dma((2, TILES)),
            dma((2,)),
            dma((NZ * NY,)),
            dma((NZ * NY,)),
            dma((2,)),
            dma,
            dma((3, 2, TILES)),
            dma((3, 2, TILES)),
            dma((TILES,)),
            dma((TILES,)),
            dma((NZ - 1, TILES)),
            dma((NZ - 1, TILES)),
            dma((NY, NW)),
            dma((NY, NW)),
        ],
        compiler_params=pltpu.CompilerParams(
            collective_id=0, has_side_effects=True, vmem_limit_bytes=48 << 20
        ),
        name="exchange",
    )(spectral_state, inverse, term_weights, legendre)


def place_kernel(column_ref, code_ref, out_ref):
    @pl.loop(0, NW)
    def _(from_w):
        for from_y in range(NY):
            column = column_ref[from_w * NY + from_y]
            last = code_ref[from_y, from_w, OWN:, :]
            moved = pltpu.roll(last, LANES - 32, 1)
            for part, rest in ((0, last), (1, moved)):
                step = span_of(rest[:, 64:65]) * (1.0 / TOP)
                main = code_ref[from_y, from_w, part * 8 : part * 8 + 8, :]
                wide = jnp.broadcast_to(step, (8, LANES))
                rows = slice(part * 8, part * 8 + 8)
                for p, value in enumerate(unpacked(main, wide)):
                    out_ref[column, p, rows, :LANES] = value
                for p, value in enumerate(unpacked(rest, wide)):
                    out_ref[column, p, rows, LANES:] = value[:, :32]


def place(slot_column, codes):
    return pl.pallas_call(
        place_kernel,
        out_shape=jax.ShapeDtypeStruct((NW * NY, 2, OWN, BAND), F32),
        in_specs=[pl.BlockSpec(memory_space=pltpu.SMEM), pl.BlockSpec(memory_space=pltpu.VMEM)],
        out_specs=pl.BlockSpec(memory_space=pltpu.VMEM),
        name="place",
    )(slot_column, codes)


def shards(spectral_state, inverse, term_weights, legendre, slot_column):
    codes = exchange(spectral_state, inverse, term_weights, legendre)
    return place(slot_column, codes)


def solution(mesh):
    placed = (
        P("wave", "term", None),
        P("term", "wave", None, None, None),
        P("term", None),
        P("wave", None, None),
        P(),
    )
    return jax.shard_map(
        shards, mesh=mesh, in_specs=placed, out_specs=P(None, None, "term", "wave"), check_vma=False
    )
```

```python
import functools

import jax
import jax.numpy as jnp
from jax import lax
from jax.experimental import pallas as pl
from jax.experimental.pallas import tpu as pltpu
from jax.sharding import PartitionSpec as P

F32 = jnp.float32
BF16 = jnp.bfloat16
I32 = jnp.int32
MESH = pl.DeviceIdType.MESH

NY, NZ, NC, NW = 4, 4, 2, 8
NDEG, NLAT = 640, 1280
OWN = 16
HALF = NDEG // NC
QUARTER = HALF // 2
LANES = 128
TILES = NDEG // LANES
MSG = QUARTER + 8
WINDOW = 384
STEPS = 8.0
TOP = 32700.0
BAND = NLAT // NW
ROWS = NY * OWN
CHUNK = 32
MEETINGS = 7


def code_of(height):
    return jnp.ceil(jnp.log2(jnp.maximum(height, 1e-30)) * STEPS).astype(I32)


def span_of(code):
    return jnp.exp2(code.astype(F32) * (1.0 / STEPS))


def gain_of(code):
    return TOP * jnp.exp2(code.astype(F32) * (-1.0 / STEPS))


def packed(real, imag, gain):
    high = (real * gain + 32768.5).astype(I32)
    low = (imag * gain + 32768.5).astype(I32)
    return lax.shift_left(high, jnp.full_like(high, 16)) | low


def unpacked(code, step):
    high = lax.shift_right_logical(code, jnp.full_like(code, 16)).astype(F32)
    low = (code & 0xFFFF).astype(F32)
    return (high - 32768.0) * step, (low - 32768.0) * step


def exchange_kernel(
    x_hbm, inv_hbm, w_hbm, leg_hbm, out_ref,
    raw_own, raw_pal, w_ref, w_pal, x_all, leg, snd, rcv, work, rhs_a, rhs_b,
    t_own, t_snd, t_rcv, z_snd, z_rcv, t_fin, grid, pieces,
    raw_own_sem, raw_pal_sem, w_sem, x_snd_sem, x_rcv_sem, x_fwd_sem, leg_sem,
    snd_sem, rcv_sem, t_snd_sem, t_rcv_sem, z_snd_sem, z_rcv_sem, f_snd_sem, f_rcv_sem, met,
):
    term = lax.axis_index("term")
    wave = lax.axis_index("wave")
    core = lax.rem(term, 2)
    y = lax.rem(term // 2, NY)
    z = term // (2 * NY)
    zy = z * NY + y

    def at(z_, y_, core_, wave_):
        return ((z_ * NY + y_) * 2 + core_, wave_)

    pal = at(z, y, 1 - core, wave)

    def own_copy(j):
        return pltpu.make_async_copy(
            inv_hbm.at[0, :, :, pl.ds(pl.multiple_of(core * HALF, 64), HALF), pl.ds(pl.multiple_of(j * LANES, LANES), LANES)],
            raw_own.at[j],
            raw_own_sem.at[j],
        )

    def pal_copy(j, d):
        slot = lax.rem(y + d, NY)
        return pltpu.make_async_remote_copy(
            src_ref=inv_hbm.at[0, slot, :, pl.ds(pl.multiple_of((1 - core) * HALF, 64), HALF), pl.ds(pl.multiple_of(j * LANES, LANES), LANES)],
            dst_ref=raw_pal.at[j, slot],
            send_sem=raw_pal_sem.at[0, j, d],
            recv_sem=raw_pal_sem.at[1, j, d],
            device_id=pal,
            device_id_type=MESH,
        )

    w_local = pltpu.make_async_copy(w_hbm, w_ref, w_sem.at[2])
    w_copy = pltpu.make_async_remote_copy(
        src_ref=w_hbm, dst_ref=w_pal, send_sem=w_sem.at[0], recv_sem=w_sem.at[1], device_id=pal, device_id_type=MESH
    )

    def x_part(z_, y_, size):
        return x_all.at[core, pl.ds(pl.multiple_of((z_ * NY + y_) * OWN, OWN), size)]

    def x_copy(dy, source):
        to_y = lax.rem(y + dy, NY)
        return pltpu.make_async_remote_copy(
            src_ref=x_hbm.at[to_y],
            dst_ref=x_part(z, source, OWN),
            send_sem=x_snd_sem.at[dy],
            recv_sem=x_rcv_sem.at[dy],
            device_id=at(z, to_y, core, wave),
            device_id_type=MESH,
        )

    def x_arrival(dy):
        return x_copy(dy, lax.rem(y + NY - dy, NY))

    def x_line_copy(dz, source):
        return pltpu.make_async_remote_copy(
            src_ref=x_part(z, 0, ROWS),
            dst_ref=x_part(source, 0, ROWS),
            send_sem=x_snd_sem.at[NY + dz],
            recv_sem=x_rcv_sem.at[NY + dz],
            device_id=at(lax.rem(z + dz, NZ), y, core, wave),
            device_id_type=MESH,
        )

    def x_line_arrival(dz):
        return x_line_copy(dz, lax.rem(z + NZ - dz, NZ))

    x_local = pltpu.make_async_copy(x_hbm.at[y], x_part(z, y, OWN), x_rcv_sem.at[0])
    x_forward = pltpu.make_async_remote_copy(
        src_ref=x_all.at[core],
        dst_ref=x_all.at[core],
        send_sem=x_fwd_sem.at[0],
        recv_sem=x_fwd_sem.at[1],
        device_id=pal,
        device_id_type=MESH,
    )
    leg_copy = pltpu.make_async_copy(leg_hbm.at[y], leg, leg_sem)

    def y_copy(kind, way, j):
        to = lax.rem(y + (1 if way == 0 else NY - 1), NY)
        return pltpu.make_async_remote_copy(
            src_ref=snd.at[kind, way, j],
            dst_ref=rcv.at[kind, way, j],
            send_sem=snd_sem.at[kind, way, j],
            recv_sem=rcv_sem.at[kind, way, j],
            device_id=at(z, to, core, wave),
            device_id_type=MESH,
        )

    def t_copy(j):
        return pltpu.make_async_remote_copy(
            src_ref=t_snd.at[j],
            dst_ref=t_rcv.at[j],
            send_sem=t_snd_sem.at[j],
            recv_sem=t_rcv_sem.at[j],
            device_id=pal,
            device_id_type=MESH,
        )

    def z_copy(i, j):
        return pltpu.make_async_remote_copy(
            src_ref=z_snd.at[i, j],
            dst_ref=z_rcv.at[i, j],
            send_sem=z_snd_sem.at[i, j],
            recv_sem=z_rcv_sem.at[i, j],
            device_id=at(lax.rem(z + 1 + i, NZ), y, core, wave),
            device_id_type=MESH,
        )

    def f_copy(dy, dw):
        to_y = lax.rem(y + dy, NY)
        to_w = lax.rem(wave + dw, NW)
        return pltpu.make_async_remote_copy(
            src_ref=pieces.at[to_y, to_w],
            dst_ref=out_ref.at[y, wave],
            send_sem=f_snd_sem.at[dy, dw],
            recv_sem=f_rcv_sem.at[dy, dw],
            device_id=at(z, to_y, core, to_w),
            device_id_type=MESH,
        )

    def f_arrival(dy, dw):
        from_y = lax.rem(y + NY - dy, NY)
        from_w = lax.rem(wave + NW - dw, NW)
        return pltpu.make_async_remote_copy(
            src_ref=pieces.at[from_y, from_w],
            dst_ref=out_ref.at[from_y, from_w],
            send_sem=f_snd_sem.at[dy, dw],
            recv_sem=f_rcv_sem.at[dy, dw],
            device_id=at(z, from_y, core, from_w),
            device_id_type=MESH,
        )

    x_forward_arrival = pltpu.make_async_remote_copy(
        src_ref=x_all.at[1 - core],
        dst_ref=x_all.at[1 - core],
        send_sem=x_fwd_sem.at[0],
        recv_sem=x_fwd_sem.at[1],
        device_id=pal,
        device_id_type=MESH,
    )

    x_pos = wave // 2
    high = lax.rem(wave, 2) * NZ + z

    def place_of(x_, y_, high_):
        return at(lax.rem(high_, NZ), y_, core, x_ * 2 + high_ // NZ)

    around = [
        place_of(lax.rem(x_pos + 1, 4), y, high),
        place_of(lax.rem(x_pos + 3, 4), y, high),
        place_of(x_pos, lax.rem(y + 1, NY), high),
        place_of(x_pos, lax.rem(y + 3, NY), high),
        place_of(x_pos, y, lax.rem(high + 1, 2 * NZ)),
        place_of(x_pos, y, lax.rem(high + 7, 2 * NZ)),
    ]

    def tell(semaphore):
        for device in around:
            pl.semaphore_signal(semaphore, inc=1, device_id=device, device_id_type=MESH)

    barrier = pltpu.get_barrier_semaphore()
    pl.semaphore_signal(barrier, inc=1, device_id=pal, device_id_type=MESH)
    tell(barrier)

    @pl.loop(0, TILES)
    def _(j):
        own_copy(j).start()

    w_local.start()
    x_local.start()
    leg_copy.start()
    pad = pl.ds(pl.multiple_of((1 - core) * HALF, 64), WINDOW - HALF)
    for side in range(2):
        rhs_a[side, pad, :] = jnp.zeros((WINDOW - HALF, 2 * LANES), BF16)
        rhs_b[side, pad, :] = jnp.zeros((WINDOW - HALF, 2 * LANES), BF16)
    grid[...] = jnp.zeros_like(grid)

    pl.semaphore_wait(barrier, 1 + len(around))
    w_copy.start()

    @pl.loop(0, TILES)
    def _(j):
        for d in (2, 1, 3, 0):
            pal_copy(j, d).start()

    tell(met.at[0])
    x_copy(1, y).start()
    x_copy(3, y).start()
    w_local.wait()
    w_copy.wait()
    weights = [w_ref[0:1, 0:1], w_ref[0:1, 1:2], w_pal[0:1, 0:1], w_pal[0:1, 1:2]]
    weights = [jnp.broadcast_to(v, (CHUNK, LANES)) for v in weights]

    def term_sum(j, slot, row):
        rows = pl.ds(row, CHUNK)
        r0 = raw_own[j, slot, 0, rows, :].astype(F32)
        j0 = raw_own[j, slot, 1, rows, :].astype(F32)
        r1 = raw_pal[j, slot, 0, rows, :].astype(F32)
        j1 = raw_pal[j, slot, 1, rows, :].astype(F32)
        a0, b0, a1, b1 = weights
        return (a0 * r0 - b0 * j0) + (a1 * r1 - b1 * j1), (a0 * j0 + b0 * r0) + (a1 * j1 + b1 * r1)

    def higher(height, real, imag):
        tall = jnp.maximum(jnp.abs(real), jnp.abs(imag))
        return jnp.maximum(height, jnp.max(tall.reshape(-1, 8, LANES), axis=0))

    def write_message(to, j, slot, half, since):
        height = jnp.zeros((8, LANES), F32)
        if since is not None:
            step = span_of(since[QUARTER : QUARTER + 8, :])[0:1] * (1.0 / TOP)
            step = jnp.broadcast_to(step, (CHUNK, LANES))
        for part in range(QUARTER // CHUNK):
            rows = slice(part * CHUNK, (part + 1) * CHUNK)
            real, imag = term_sum(j, slot, half * QUARTER + part * CHUNK)
            if since is not None:
                more_real, more_imag = unpacked(since[rows, :], step)
                real, imag = real + more_real, imag + more_imag
            work[0, rows, :] = real
            work[1, rows, :] = imag
            height = higher(height, real, imag)
        height = jnp.broadcast_to(jnp.max(height, axis=0, keepdims=True), (8, LANES))
        code = code_of(height)
        gain = jnp.broadcast_to(gain_of(code)[0:1], (CHUNK, LANES))
        for part in range(QUARTER // CHUNK):
            rows = slice(part * CHUNK, (part + 1) * CHUNK)
            to[rows, :] = packed(work[0, rows, :], work[1, rows, :], gain)
        to[QUARTER : QUARTER + 8, :] = code

    def stage_first(j):
        own_copy(j).wait()
        pal_copy(j, 2).wait_recv()
        for way in range(2):
            write_message(snd.at[0, way, j], j, lax.rem(y + 2, NY), way, None)
            y_copy(0, way, j).start()
        for way in range(2):
            slot = lax.rem(y + (1 if way == 0 else NY - 1), NY)
            pal_copy(j, 1 if way == 0 else NY - 1).wait_recv()
            write_message(snd.at[1, way, j], j, slot, 1 - way, None)
            y_copy(1, way, j).start()

    def stage_sum(j):
        for way in range(2):
            slot = lax.rem(y + (1 if way == 0 else NY - 1), NY)
            y_copy(0, way, j).wait_recv()
            write_message(snd.at[2, way, j], j, slot, way, rcv.at[0, way, j])
            y_copy(2, way, j).start()

    def stage_product(j):
        pal_copy(j, 0).wait_recv()
        for kind in (1, 2):
            for way in range(2):
                y_copy(kind, way, j).wait_recv()
        for half in range(2):
            first = rcv.at[2, half, j]
            second = rcv.at[1, 1 - half, j]
            steps = [
                jnp.broadcast_to(span_of(part[QUARTER : QUARTER + 8, :])[0:1] * (1.0 / TOP), (CHUNK, LANES))
                for part in (first, second)
            ]
            for part in range(QUARTER // CHUNK):
                rows = slice(part * CHUNK, (part + 1) * CHUNK)
                start = half * QUARTER + part * CHUNK
                real, imag = term_sum(j, y, start)
                for source, step in zip((first, second), steps):
                    more_real, more_imag = unpacked(source[rows, :], step)
                    real, imag = real + more_real, imag + more_imag
                real_high = real.astype(BF16)
                imag_high = imag.astype(BF16)
                real_low = (real - real_high.astype(F32)).astype(BF16)
                imag_low = (imag - imag_high.astype(F32)).astype(BF16)
                into = pl.ds(pl.multiple_of(core * (WINDOW - HALF) + start, CHUNK), CHUNK)
                rhs_a[0, into, :] = jnp.concatenate([real_high, imag_high], axis=1)
                rhs_a[1, into, :] = jnp.concatenate([real_low, imag_low], axis=1)
                rhs_b[0, into, :] = jnp.concatenate([-imag_high, real_high], axis=1)
                rhs_b[1, into, :] = jnp.concatenate([-imag_low, real_low], axis=1)

        def product(owner, row):
            rows = pl.ds(pl.multiple_of(row, 128), 128)
            left = x_all[owner, rows, pl.ds(pl.multiple_of(core * 256, LANES), WINDOW)]
            right = x_all[owner, rows, pl.ds(pl.multiple_of(NDEG + core * 256, LANES), WINDOW)]
            value = jnp.dot(left, rhs_a[0], preferred_element_type=F32)
            value += jnp.dot(right, rhs_b[0], preferred_element_type=F32)
            value += jnp.dot(left, rhs_a[1], preferred_element_type=F32)
            value += jnp.dot(right, rhs_b[1], preferred_element_type=F32)
            return value

        @pl.loop(0, 2)
        def _(i):
            t_snd[j, pl.ds(pl.multiple_of(i * 128, 128), 128), :] = product(1 - core, i * 128)

        t_copy(j).start()

        @pl.loop(0, 2)
        def _(i):
            t_own[j, pl.ds(pl.multiple_of(i * 128, 128), 128), :] = product(core, i * 128)

    def stage_spread(j):
        t_copy(j).wait_recv()
        for i in range(NZ):
            to = lax.rem(z + 1 + i, NZ)
            rows = pl.ds(pl.multiple_of(to * ROWS, ROWS), ROWS)
            value = t_own[j, rows, :] + t_rcv[j, rows, :]
            if i == NZ - 1:
                t_fin[j] = value
                continue
            real, imag = value[:, :LANES], value[:, LANES:]
            height = higher(jnp.zeros((8, LANES), F32), real, imag)
            height = jnp.broadcast_to(jnp.max(height, axis=0, keepdims=True), (8, LANES))
            code = code_of(height)
            gain = jnp.broadcast_to(gain_of(code)[0:1], (ROWS, LANES))
            z_snd[i, j, :ROWS, :] = packed(real, imag, gain)
            z_snd[i, j, ROWS:, :] = code
            z_copy(i, j).start()

    def stage_synthesis(j):
        value = t_fin[j]
        real, imag = value[:, :LANES], value[:, LANES:]
        for i in range(NZ - 1):
            z_copy(i, j).wait_recv()
            step = span_of(z_rcv[i, j, ROWS:, :])[0:1] * (1.0 / TOP)
            step = jnp.broadcast_to(step, (ROWS, LANES))
            more_real, more_imag = unpacked(z_rcv[i, j, :ROWS, :], step)
            real, imag = real + more_real, imag + more_imag
        both = jnp.concatenate([real, imag], axis=0)
        high = both.astype(BF16)
        low = (both - high.astype(F32)).astype(BF16)
        left = jnp.concatenate([high, low], axis=0)
        table = pl.ds(pl.multiple_of(j * LANES, LANES), LANES)

        @pl.loop(0, NLAT // 256)
        def _(i):
            columns = pl.ds(pl.multiple_of(i * 256, 256), 256)
            value = jnp.dot(left, leg[table, columns], preferred_element_type=F32)
            grid[:, columns] += value[: 2 * ROWS] + value[2 * ROWS :]

    @pl.loop(0, TILES + 5)
    def _(it):
        @pl.when(it < TILES)
        def _():
            stage_first(it)

        @pl.when((it >= 1) & (it < TILES + 1))
        def _():
            stage_sum(it - 1)

        @pl.when(it < MEETINGS)
        def _():
            pl.semaphore_wait(met.at[it], len(around))

        @pl.when(it < MEETINGS - 1)
        def _():
            tell(met.at[it + 1])

        @pl.when(it == 0)
        def _():
            x_copy(2, y).start()

        @pl.when(it == 1)
        def _():
            x_local.wait()
            for dy in range(1, NY):
                x_arrival(dy).wait_recv()
            for dz in (2, 1, 3):
                x_line_copy(dz, z).start()

        @pl.when(it == 3)
        def _():
            for dz in (2, 1, 3):
                x_line_arrival(dz).wait_recv()
            x_forward.start()
            x_forward_arrival.wait_recv()

        @pl.when((it >= 3) & (it < TILES + 3))
        def _():
            stage_product(it - 3)

        @pl.when((it >= 4) & (it < TILES + 4))
        def _():
            stage_spread(it - 4)

        @pl.when(it == 5)
        def _():
            leg_copy.wait()

        @pl.when(it >= 5)
        def _():
            stage_synthesis(it - 5)

    lane = lax.broadcasted_iota(I32, (8, LANES), 1)
    for to_y in range(NY):
        rows = slice(to_y * OWN, (to_y + 1) * OWN)
        real = grid[rows, :]
        imag = grid[ROWS + to_y * OWN : ROWS + (to_y + 1) * OWN, :]
        height = jnp.max(jnp.maximum(jnp.abs(real), jnp.abs(imag)), axis=1, keepdims=True)
        code = code_of(jnp.broadcast_to(height, (OWN, LANES)))
        gain = gain_of(code)
        gain = jnp.concatenate([gain] * (NLAT // LANES), axis=1)
        value = packed(real, imag, gain)
        for to_w in range(NW):
            tile, skip = divmod(to_w * BAND, LANES)
            band = value[:, tile * LANES : tile * LANES + 2 * LANES]
            if skip:
                band = pltpu.roll(band, 2 * LANES - skip, 1)
            rest = band[:, LANES:]
            last = jnp.where(lane < 96, code[:8], code[8:])
            last = jnp.where(lane < 64, pltpu.roll(rest[8:], 32, 1), last)
            last = jnp.where(lane < 32, rest[:8], last)
            pieces[to_y, to_w, :OWN, :] = band[:, :LANES]
            pieces[to_y, to_w, OWN:, :] = last

        dy = lax.rem(to_y + NY - y, NY)
        for dw in (1, 7, 3, 5, 2, 6, 4):
            f_copy(dy, dw).start()

        @pl.when(dy != 0)
        def _():
            f_copy(dy, 0).start()


    stay = pltpu.make_async_copy(pieces.at[y, wave], out_ref.at[y, wave], f_rcv_sem.at[0, 0])
    stay.start()

    @pl.loop(0, TILES)
    def _(j):
        for d in range(NY):
            pal_copy(j, d).wait_send()
        t_copy(j).wait_send()
        for kind in range(3):
            for way in range(2):
                y_copy(kind, way, j).wait_send()
        for i in range(NZ - 1):
            z_copy(i, j).wait_send()

    for d in range(1, NY):
        x_copy(d, y).wait_send()
        x_line_copy(d, z).wait_send()
    x_forward.wait_send()
    stay.wait()

    @pl.loop(1, NW)
    def _(dw):
        @pl.loop(0, NY)
        def _(dy):
            f_arrival(dy, dw).wait_recv()
            f_copy(dy, dw).wait_send()

    @pl.loop(1, NY)
    def _(dy):
        f_arrival(dy, 0).wait_recv()
        f_copy(dy, 0).wait_send()


def exchange(spectral_state, inverse, term_weights, legendre):
    any_space = pl.BlockSpec(memory_space=pl.ANY)
    dma = pltpu.SemaphoreType.DMA
    return pl.pallas_call(
        exchange_kernel,
        out_shape=jax.ShapeDtypeStruct((NY, NW, OWN + 8, LANES), I32),
        in_specs=[any_space] * 4,
        out_specs=any_space,
        scratch_shapes=[
            pltpu.VMEM((TILES, NY, 2, HALF, LANES), BF16),
            pltpu.VMEM((TILES, NY, 2, HALF, LANES), BF16),
            pltpu.VMEM((1, 2), F32),
            pltpu.VMEM((1, 2), F32),
            pltpu.VMEM((2, NZ * NY * OWN, 2 * NDEG), BF16),
            pltpu.VMEM((NDEG, NLAT), BF16),
            pltpu.VMEM((3, 2, TILES, MSG, LANES), I32),
            pltpu.VMEM((3, 2, TILES, MSG, LANES), I32),
            pltpu.VMEM((2, QUARTER, LANES), F32),
            pltpu.VMEM((2, WINDOW, 2 * LANES), BF16),
            pltpu.VMEM((2, WINDOW, 2 * LANES), BF16),
            pltpu.VMEM((TILES, 256, 2 * LANES), F32),
            pltpu.VMEM((TILES, 256, 2 * LANES), F32),
            pltpu.VMEM((TILES, 256, 2 * LANES), F32),
            pltpu.VMEM((NZ - 1, TILES, ROWS + 8, LANES), I32),
            pltpu.VMEM((NZ - 1, TILES, ROWS + 8, LANES), I32),
            pltpu.VMEM((TILES, ROWS, 2 * LANES), F32),
            pltpu.VMEM((2 * ROWS, NLAT), F32),
            pltpu.VMEM((NY, NW, OWN + 8, LANES), I32),
            dma((TILES,)),
            dma((2, TILES, NY)),
            dma((3,)),
            dma((2 * NY,)),
            dma((2 * NY,)),
            dma((2,)),
            dma,
            dma((3, 2, TILES)),
            dma((3, 2, TILES)),
            dma((TILES,)),
            dma((TILES,)),
            dma((NZ - 1, TILES)),
            dma((NZ - 1, TILES)),
            dma((NY, NW)),
            dma((NY, NW)),
            pltpu.SemaphoreType.REGULAR((MEETINGS,)),
        ],
        compiler_params=pltpu.CompilerParams(
            collective_id=0, has_side_effects=True, vmem_limit_bytes=60 * 1024 * 1024
        ),
        name="exchange",
    )(spectral_state, inverse, term_weights, legendre)


def place_kernel(column_ref, code_ref, out_hbm, decoded, sem):
    def out_copy(slot):
        return pltpu.make_async_copy(decoded.at[slot], out_hbm.at[column_ref[slot]], sem.at[slot])

    @pl.loop(0, NW)
    def _(from_w):
        for from_y in range(NY):
            slot = from_w * NY + from_y
            last = code_ref[from_y, from_w, OWN:, :]
            moved = pltpu.roll(last, LANES - 32, 1)
            for part, rest in ((0, last), (1, moved)):
                step = span_of(rest[:, 64:65]) * (1.0 / TOP)
                main = code_ref[from_y, from_w, part * 8 : part * 8 + 8, :]
                wide = jnp.broadcast_to(step, (8, LANES))
                rows = slice(part * 8, part * 8 + 8)
                for p, value in enumerate(unpacked(main, wide)):
                    decoded[slot, p, rows, :LANES] = value
                for p, value in enumerate(unpacked(rest, wide)):
                    decoded[slot, p, rows, LANES:] = value[:, :32]
            out_copy(slot).start()

    @pl.loop(0, NW * NY)
    def _(slot):
        out_copy(slot).wait()


def place(slot_column, codes):
    shape = (NW * NY, 2, OWN, BAND)
    return pl.pallas_call(
        place_kernel,
        out_shape=jax.ShapeDtypeStruct(shape, F32),
        in_specs=[pl.BlockSpec(memory_space=pltpu.SMEM), pl.BlockSpec(memory_space=pltpu.VMEM)],
        out_specs=pl.BlockSpec(memory_space=pl.ANY),
        scratch_shapes=[pltpu.VMEM(shape, F32), pltpu.SemaphoreType.DMA((NW * NY,))],
        compiler_params=pltpu.CompilerParams(vmem_limit_bytes=60 * 1024 * 1024),
        name="place",
    )(slot_column, codes)


def shards(spectral_state, inverse, term_weights, legendre, slot_column):
    codes = exchange(spectral_state, inverse, term_weights, legendre)
    return place(slot_column, codes)


def solution(mesh):
    placed = (
        P("wave", "term", None),
        P("term", "wave", None, None, None),
        P("term", None),
        P("wave", None, None),
        P(),
    )
    return jax.shard_map(
        shards, mesh=mesh, in_specs=placed, out_specs=P(None, None, "term", "wave"), check_vma=False
    )
```

```python
import functools

import jax
import jax.numpy as jnp
from jax import lax
from jax.experimental import pallas as pl
from jax.experimental.pallas import tpu as pltpu
from jax.sharding import PartitionSpec as P

F32 = jnp.float32
BF16 = jnp.bfloat16
I32 = jnp.int32
MESH = pl.DeviceIdType.MESH

NY, NZ, NC, NW = 4, 4, 2, 8
NDEG, NLAT = 640, 1280
OWN = 16
HALF = NDEG // NC
QUARTER = HALF // 2
LANES = 128
TILES = NDEG // LANES
MSG = QUARTER + 8
WINDOW = 384
STEPS = 8.0
TOP = 32700.0
BAND = NLAT // NW
ROWS = NY * OWN
CHUNK = 32
MEETINGS = 7


def code_of(height):
    return jnp.ceil(jnp.log2(jnp.maximum(height, 1e-30)) * STEPS).astype(I32)


def span_of(code):
    return jnp.exp2(code.astype(F32) * (1.0 / STEPS))


def gain_of(code):
    return TOP * jnp.exp2(code.astype(F32) * (-1.0 / STEPS))


def packed(real, imag, gain):
    high = (real * gain + 32768.5).astype(I32)
    low = (imag * gain + 32768.5).astype(I32)
    return lax.shift_left(high, jnp.full_like(high, 16)) | low


def unpacked(code, step):
    high = lax.shift_right_logical(code, jnp.full_like(code, 16)).astype(F32)
    low = (code & 0xFFFF).astype(F32)
    return (high - 32768.0) * step, (low - 32768.0) * step


def exchange_kernel(
    x_hbm, inv_hbm, w_hbm, leg_hbm, out_ref,
    raw_own, raw_pal, w_ref, w_pal, x_all, leg, snd, rcv, work, rhs,
    t_own, t_snd, t_rcv, z_snd, z_rcv, t_fin, grid, pieces,
    raw_own_sem, raw_pal_sem, w_sem, x_snd_sem, x_rcv_sem, x_fwd_sem, leg_sem,
    snd_sem, rcv_sem, t_snd_sem, t_rcv_sem, z_snd_sem, z_rcv_sem, f_snd_sem, f_rcv_sem, met,
):
    term = lax.axis_index("term")
    wave = lax.axis_index("wave")
    core = lax.rem(term, 2)
    y = lax.rem(term // 2, NY)
    z = term // (2 * NY)
    zy = z * NY + y

    def at(z_, y_, core_, wave_):
        return ((z_ * NY + y_) * 2 + core_, wave_)

    pal = at(z, y, 1 - core, wave)

    def own_copy(j):
        return pltpu.make_async_copy(
            inv_hbm.at[0, :, :, pl.ds(pl.multiple_of(core * HALF, 64), HALF), pl.ds(pl.multiple_of(j * LANES, LANES), LANES)],
            raw_own.at[j],
            raw_own_sem.at[j],
        )

    def pal_copy(j, d):
        slot = lax.rem(y + d, NY)
        return pltpu.make_async_remote_copy(
            src_ref=inv_hbm.at[0, slot, :, pl.ds(pl.multiple_of((1 - core) * HALF, 64), HALF), pl.ds(pl.multiple_of(j * LANES, LANES), LANES)],
            dst_ref=raw_pal.at[j, slot],
            send_sem=raw_pal_sem.at[0, j, d],
            recv_sem=raw_pal_sem.at[1, j, d],
            device_id=pal,
            device_id_type=MESH,
        )

    w_local = pltpu.make_async_copy(w_hbm, w_ref, w_sem.at[2])
    w_copy = pltpu.make_async_remote_copy(
        src_ref=w_hbm, dst_ref=w_pal, send_sem=w_sem.at[0], recv_sem=w_sem.at[1], device_id=pal, device_id_type=MESH
    )

    def x_part(z_, y_, size):
        return x_all.at[core, pl.ds(pl.multiple_of((z_ * NY + y_) * OWN, OWN), size)]

    def x_copy(dy, source):
        to_y = lax.rem(y + dy, NY)
        return pltpu.make_async_remote_copy(
            src_ref=x_hbm.at[to_y],
            dst_ref=x_part(z, source, OWN),
            send_sem=x_snd_sem.at[dy],
            recv_sem=x_rcv_sem.at[dy],
            device_id=at(z, to_y, core, wave),
            device_id_type=MESH,
        )

    def x_arrival(dy):
        return x_copy(dy, lax.rem(y + NY - dy, NY))

    def x_line_copy(way, hop):
        owner = z + (-hop if way == 0 else hop)
        to_z = z + (1 if way == 0 else -1)
        copy = pltpu.make_async_remote_copy(
            src_ref=x_part(owner, 0, ROWS),
            dst_ref=x_part(owner, 0, ROWS),
            send_sem=x_snd_sem.at[NY + 3 * way + hop],
            recv_sem=x_rcv_sem.at[NY + 3 * way + hop],
            device_id=at(to_z, y, core, wave),
            device_id_type=MESH,
        )
        inside = (owner >= 0) & (to_z < NZ) if way == 0 else (owner < NZ) & (to_z >= 0)
        return copy, inside

    def x_line_arrival(way, hop):
        owner = z + (-1 - hop if way == 0 else 1 + hop)
        copy = pltpu.make_async_remote_copy(
            src_ref=x_part(owner, 0, ROWS),
            dst_ref=x_part(owner, 0, ROWS),
            send_sem=x_snd_sem.at[NY + 3 * way + hop],
            recv_sem=x_rcv_sem.at[NY + 3 * way + hop],
            device_id=pal,
            device_id_type=MESH,
        )
        return copy, owner, (owner >= 0) if way == 0 else (owner < NZ)

    def x_pass(owner, owner_core):
        part = x_all.at[owner_core, pl.ds(pl.multiple_of(owner * ROWS, ROWS), ROWS)]
        return pltpu.make_async_remote_copy(
            src_ref=part,
            dst_ref=part,
            send_sem=x_fwd_sem.at[0, owner],
            recv_sem=x_fwd_sem.at[1, owner],
            device_id=pal,
            device_id_type=MESH,
        )

    def x_line_send(hop):
        for way in range(2):
            copy, inside = x_line_copy(way, hop)
            pl.when(inside)(copy.start)

    def x_line_take(hop):
        for way in range(2):
            copy, owner, present = x_line_arrival(way, hop)

            @pl.when(present)
            def _():
                copy.wait_recv()
                x_pass(owner, core).start()

    x_local = pltpu.make_async_copy(x_hbm.at[y], x_part(z, y, OWN), x_rcv_sem.at[0])
    leg_copy = pltpu.make_async_copy(leg_hbm.at[y], leg, leg_sem)

    def y_copy(kind, way, j):
        to = lax.rem(y + (1 if way == 0 else NY - 1), NY)
        return pltpu.make_async_remote_copy(
            src_ref=snd.at[kind, way, j],
            dst_ref=rcv.at[kind, way, j],
            send_sem=snd_sem.at[kind, way, j],
            recv_sem=rcv_sem.at[kind, way, j],
            device_id=at(z, to, core, wave),
            device_id_type=MESH,
        )

    def t_copy(j):
        return pltpu.make_async_remote_copy(
            src_ref=t_snd.at[j],
            dst_ref=t_rcv.at[j],
            send_sem=t_snd_sem.at[j],
            recv_sem=t_rcv_sem.at[j],
            device_id=pal,
            device_id_type=MESH,
        )

    def z_copy(i, j):
        return pltpu.make_async_remote_copy(
            src_ref=z_snd.at[i, j],
            dst_ref=z_rcv.at[i, j],
            send_sem=z_snd_sem.at[i, j],
            recv_sem=z_rcv_sem.at[i, j],
            device_id=at(lax.rem(z + 1 + i, NZ), y, core, wave),
            device_id_type=MESH,
        )

    def shifted(z_, steps):
        return lax.rem(z_ + steps, NZ)

    block = shifted(z, 1 + 2 * core)
    origin = shifted(z, 3 - 2 * core)

    def f_copy(dy, dw):
        to_y = lax.rem(y + dy, NY)
        to_w = lax.rem(wave + dw, NW)
        return pltpu.make_async_remote_copy(
            src_ref=pieces.at[to_y, to_w],
            dst_ref=out_ref.at[y, wave],
            send_sem=f_snd_sem.at[dy, dw],
            recv_sem=f_rcv_sem.at[dy, dw],
            device_id=at(block, to_y, core, to_w),
            device_id_type=MESH,
        )

    def f_arrival(dy, dw):
        from_y = lax.rem(y + NY - dy, NY)
        from_w = lax.rem(wave + NW - dw, NW)
        return pltpu.make_async_remote_copy(
            src_ref=pieces.at[from_y, from_w],
            dst_ref=out_ref.at[from_y, from_w],
            send_sem=f_snd_sem.at[dy, dw],
            recv_sem=f_rcv_sem.at[dy, dw],
            device_id=at(origin, from_y, core, from_w),
            device_id_type=MESH,
        )

    x_pos = wave // 2
    high = lax.rem(wave, 2) * NZ + z

    def place_of(x_, y_, high_):
        return at(lax.rem(high_, NZ), y_, core, x_ * 2 + high_ // NZ)

    around = [
        place_of(lax.rem(x_pos + 1, 4), y, high),
        place_of(lax.rem(x_pos + 3, 4), y, high),
        place_of(x_pos, lax.rem(y + 1, NY), high),
        place_of(x_pos, lax.rem(y + 3, NY), high),
        place_of(x_pos, y, lax.rem(high + 1, 2 * NZ)),
        place_of(x_pos, y, lax.rem(high + 7, 2 * NZ)),
    ]

    def tell(semaphore):
        for device in around:
            pl.semaphore_signal(semaphore, inc=1, device_id=device, device_id_type=MESH)

    barrier = pltpu.get_barrier_semaphore()
    pl.semaphore_signal(barrier, inc=1, device_id=pal, device_id_type=MESH)
    tell(barrier)

    @pl.loop(0, TILES)
    def _(j):
        own_copy(j).start()

    w_local.start()
    x_local.start()
    leg_copy.start()
    for side in range(2):
        for base in (0, WINDOW):
            pad = pl.ds(pl.multiple_of(base + (1 - core) * HALF, 64), WINDOW - HALF)
            rhs[side, pad, :] = jnp.zeros((WINDOW - HALF, 2 * LANES), BF16)
    grid[...] = jnp.zeros_like(grid)

    pl.semaphore_wait(barrier, 1 + len(around))
    w_copy.start()

    @pl.loop(0, TILES)
    def _(j):
        for d in (2, 1, 3, 0):
            pal_copy(j, d).start()

    tell(met.at[0])
    x_copy(1, y).start()
    x_copy(3, y).start()
    pl.semaphore_wait(met.at[0], len(around))
    tell(met.at[1])
    x_copy(2, y).start()
    w_local.wait()
    w_copy.wait()
    weights = [w_ref[0:1, 0:1], w_ref[0:1, 1:2], w_pal[0:1, 0:1], w_pal[0:1, 1:2]]
    weights = [jnp.broadcast_to(v, (CHUNK, LANES)) for v in weights]

    def term_sum(j, slot, row):
        rows = pl.ds(row, CHUNK)
        r0 = raw_own[j, slot, 0, rows, :].astype(F32)
        j0 = raw_own[j, slot, 1, rows, :].astype(F32)
        r1 = raw_pal[j, slot, 0, rows, :].astype(F32)
        j1 = raw_pal[j, slot, 1, rows, :].astype(F32)
        a0, b0, a1, b1 = weights
        return (a0 * r0 - b0 * j0) + (a1 * r1 - b1 * j1), (a0 * j0 + b0 * r0) + (a1 * j1 + b1 * r1)

    def higher(height, real, imag):
        tall = jnp.maximum(jnp.abs(real), jnp.abs(imag))
        return jnp.maximum(height, jnp.max(tall.reshape(-1, 8, LANES), axis=0))

    def write_message(to, j, slot, half, since):
        height = jnp.zeros((8, LANES), F32)
        if since is not None:
            step = span_of(since[QUARTER : QUARTER + 8, :])[0:1] * (1.0 / TOP)
            step = jnp.broadcast_to(step, (CHUNK, LANES))
        for part in range(QUARTER // CHUNK):
            rows = slice(part * CHUNK, (part + 1) * CHUNK)
            real, imag = term_sum(j, slot, half * QUARTER + part * CHUNK)
            if since is not None:
                more_real, more_imag = unpacked(since[rows, :], step)
                real, imag = real + more_real, imag + more_imag
            work[0, rows, :] = real
            work[1, rows, :] = imag
            height = higher(height, real, imag)
        height = jnp.broadcast_to(jnp.max(height, axis=0, keepdims=True), (8, LANES))
        code = code_of(height)
        gain = jnp.broadcast_to(gain_of(code)[0:1], (CHUNK, LANES))
        for part in range(QUARTER // CHUNK):
            rows = slice(part * CHUNK, (part + 1) * CHUNK)
            to[rows, :] = packed(work[0, rows, :], work[1, rows, :], gain)
        to[QUARTER : QUARTER + 8, :] = code

    def stage_first(j):
        own_copy(j).wait()
        pal_copy(j, 2).wait_recv()
        for way in range(2):
            write_message(snd.at[0, way, j], j, lax.rem(y + 2, NY), way, None)
            y_copy(0, way, j).start()

    def stage_own(j):
        for way in range(2):
            slot = lax.rem(y + (1 if way == 0 else NY - 1), NY)
            pal_copy(j, 1 if way == 0 else NY - 1).wait_recv()
            write_message(snd.at[1, way, j], j, slot, 1 - way, None)
            y_copy(1, way, j).start()

    def stage_sum(j):
        for way in range(2):
            slot = lax.rem(y + (1 if way == 0 else NY - 1), NY)
            y_copy(0, way, j).wait_recv()
            write_message(snd.at[2, way, j], j, slot, way, rcv.at[0, way, j])
            y_copy(2, way, j).start()

    def stage_product(j):
        pal_copy(j, 0).wait_recv()
        for kind in (1, 2):
            for way in range(2):
                y_copy(kind, way, j).wait_recv()
        for half in range(2):
            first = rcv.at[2, half, j]
            second = rcv.at[1, 1 - half, j]
            steps = [
                jnp.broadcast_to(span_of(part[QUARTER : QUARTER + 8, :])[0:1] * (1.0 / TOP), (CHUNK, LANES))
                for part in (first, second)
            ]
            for part in range(QUARTER // CHUNK):
                rows = slice(part * CHUNK, (part + 1) * CHUNK)
                start = half * QUARTER + part * CHUNK
                real, imag = term_sum(j, y, start)
                for source, step in zip((first, second), steps):
                    more_real, more_imag = unpacked(source[rows, :], step)
                    real, imag = real + more_real, imag + more_imag
                real_high = real.astype(BF16)
                imag_high = imag.astype(BF16)
                real_low = (real - real_high.astype(F32)).astype(BF16)
                imag_low = (imag - imag_high.astype(F32)).astype(BF16)
                into = pl.ds(pl.multiple_of(core * (WINDOW - HALF) + start, CHUNK), CHUNK)
                also = pl.ds(pl.multiple_of(WINDOW + core * (WINDOW - HALF) + start, CHUNK), CHUNK)
                rhs[0, into, :] = jnp.concatenate([real_high, imag_high], axis=1)
                rhs[1, into, :] = jnp.concatenate([real_low, imag_low], axis=1)
                rhs[0, also, :] = jnp.concatenate([-imag_high, real_high], axis=1)
                rhs[1, also, :] = jnp.concatenate([-imag_low, real_low], axis=1)

        def product(owner):
            left = x_all[owner, :, pl.ds(pl.multiple_of(core * 256, LANES), WINDOW)]
            right = x_all[owner, :, pl.ds(pl.multiple_of(NDEG + core * 256, LANES), WINDOW)]
            both = jnp.concatenate([left, right], axis=1)
            value = jnp.dot(both, rhs[0], preferred_element_type=F32)
            return value + jnp.dot(both, rhs[1], preferred_element_type=F32)

        t_snd[j] = product(1 - core)
        t_copy(j).start()
        t_own[j] = product(core)

    def stage_spread(j):
        t_copy(j).wait_recv()
        for i in range(NZ):
            to = lax.rem(z + 1 + i, NZ)
            rows = pl.ds(pl.multiple_of(shifted(to, 1 + 2 * core) * ROWS, ROWS), ROWS)
            value = t_own[j, rows, :] + t_rcv[j, rows, :]
            if i == NZ - 1:
                t_fin[j] = value
                continue
            real, imag = value[:, :LANES], value[:, LANES:]
            height = higher(jnp.zeros((8, LANES), F32), real, imag)
            height = jnp.broadcast_to(jnp.max(height, axis=0, keepdims=True), (8, LANES))
            code = code_of(height)
            gain = jnp.broadcast_to(gain_of(code)[0:1], (ROWS, LANES))
            z_snd[i, j, :ROWS, :] = packed(real, imag, gain)
            z_snd[i, j, ROWS:, :] = code
            z_copy(i, j).start()

    def stage_synthesis(j):
        value = t_fin[j]
        real, imag = value[:, :LANES], value[:, LANES:]
        for i in range(NZ - 1):
            z_copy(i, j).wait_recv()
            step = span_of(z_rcv[i, j, ROWS:, :])[0:1] * (1.0 / TOP)
            step = jnp.broadcast_to(step, (ROWS, LANES))
            more_real, more_imag = unpacked(z_rcv[i, j, :ROWS, :], step)
            real, imag = real + more_real, imag + more_imag
        both = jnp.concatenate([real, imag], axis=0)
        high = both.astype(BF16)
        low = (both - high.astype(F32)).astype(BF16)
        left = jnp.concatenate([high, low], axis=0)
        table = pl.ds(pl.multiple_of(j * LANES, LANES), LANES)

        @pl.loop(0, NLAT // 256)
        def _(i):
            columns = pl.ds(pl.multiple_of(i * 256, 256), 256)
            value = jnp.dot(left, leg[table, columns], preferred_element_type=F32)
            grid[:, columns] += value[: 2 * ROWS] + value[2 * ROWS :]

    @pl.loop(0, TILES + 2)
    def _(it):
        @pl.when(it < TILES)
        def _():
            stage_first(it)

        @pl.when((it >= 1) & (it < TILES + 1))
        def _():
            stage_sum(it - 1)

        @pl.when(it < TILES)
        def _():
            stage_own(it)

        @pl.when(it < MEETINGS - 1)
        def _():
            pl.semaphore_wait(met.at[it + 1], len(around))

        @pl.when(it < MEETINGS - 2)
        def _():
            tell(met.at[it + 2])

        @pl.when(it == 0)
        def _():
            x_local.wait()
            for dy in range(1, NY):
                x_arrival(dy).wait_recv()
            x_line_send(0)
            x_pass(z, core).start()

        @pl.when(it == 1)
        def _():
            x_line_take(0)
            x_line_send(1)

        @pl.when(it == 2)
        def _():
            x_line_take(1)
            x_line_send(2)

        @pl.when(it == 3)
        def _():
            x_line_take(2)
            for owner in range(NZ):
                x_pass(owner, 1 - core).wait_recv()

        @pl.when(it >= 3)
        def _():
            @pl.loop(jnp.where(it == 3, 0, it - 2), it - 1)
            def _(j):
                stage_product(j)
                stage_spread(j)

        @pl.when(it == 4)
        def _():
            leg_copy.wait()

        @pl.when(it >= 4)
        def _():
            @pl.loop(
                jnp.where(it == 4, 0, it - 3), jnp.where(it == TILES + 1, TILES, it - 2)
            )
            def _(j):
                stage_synthesis(j)

    lane = lax.broadcasted_iota(I32, (8, LANES), 1)
    @pl.loop(0, NY)
    def _(turn):
        dy = jnp.where(turn < 3, jnp.where(turn < 1, 2, turn * 2 - 1), 0)
        to_y = lax.rem(y + dy, NY)
        real = grid[pl.ds(pl.multiple_of(to_y * OWN, OWN), OWN), :]
        imag = grid[pl.ds(pl.multiple_of(ROWS + to_y * OWN, OWN), OWN), :]
        height = jnp.max(jnp.maximum(jnp.abs(real), jnp.abs(imag)), axis=1, keepdims=True)
        code = code_of(jnp.broadcast_to(height, (OWN, LANES)))
        gain = gain_of(code)
        gain = jnp.concatenate([gain] * (NLAT // LANES), axis=1)
        value = packed(real, imag, gain)
        for to_w in range(NW):
            tile, skip = divmod(to_w * BAND, LANES)
            band = value[:, tile * LANES : tile * LANES + 2 * LANES]
            if skip:
                band = pltpu.roll(band, 2 * LANES - skip, 1)
            rest = band[:, LANES:]
            last = jnp.where(lane < 96, code[:8], code[8:])
            last = jnp.where(lane < 64, pltpu.roll(rest[8:], 32, 1), last)
            last = jnp.where(lane < 32, rest[:8], last)
            pieces[to_y, to_w, :OWN, :] = band[:, :LANES]
            pieces[to_y, to_w, OWN:, :] = last

        for dw in (5, 3, 1, 7, 4, 2, 6, 0):
            f_copy(dy, dw).start()


    @pl.loop(0, TILES)
    def _(j):
        for d in range(NY):
            pal_copy(j, d).wait_send()
        t_copy(j).wait_send()
        for kind in range(3):
            for way in range(2):
                y_copy(kind, way, j).wait_send()
        for i in range(NZ - 1):
            z_copy(i, j).wait_send()

    for d in range(1, NY):
        x_copy(d, y).wait_send()
    for hop in range(3):
        for way in range(2):
            copy, inside = x_line_copy(way, hop)
            pl.when(inside)(copy.wait_send)
    for owner in range(NZ):
        x_pass(owner, core).wait_send()

    @pl.loop(0, NW)
    def _(dw):
        @pl.loop(0, NY)
        def _(dy):
            f_arrival(dy, dw).wait_recv()
            f_copy(dy, dw).wait_send()


def exchange(spectral_state, inverse, term_weights, legendre):
    any_space = pl.BlockSpec(memory_space=pl.ANY)
    dma = pltpu.SemaphoreType.DMA
    return pl.pallas_call(
        exchange_kernel,
        out_shape=jax.ShapeDtypeStruct((NY, NW, OWN + 8, LANES), I32),
        in_specs=[any_space] * 4,
        out_specs=any_space,
        scratch_shapes=[
            pltpu.VMEM((TILES, NY, 2, HALF, LANES), BF16),
            pltpu.VMEM((TILES, NY, 2, HALF, LANES), BF16),
            pltpu.VMEM((1, 2), F32),
            pltpu.VMEM((1, 2), F32),
            pltpu.VMEM((2, NZ * NY * OWN, 2 * NDEG), BF16),
            pltpu.VMEM((NDEG, NLAT), BF16),
            pltpu.VMEM((3, 2, TILES, MSG, LANES), I32),
            pltpu.VMEM((3, 2, TILES, MSG, LANES), I32),
            pltpu.VMEM((2, QUARTER, LANES), F32),
            pltpu.VMEM((2, 2 * WINDOW, 2 * LANES), BF16),
            pltpu.VMEM((TILES, 256, 2 * LANES), F32),
            pltpu.VMEM((TILES, 256, 2 * LANES), F32),
            pltpu.VMEM((TILES, 256, 2 * LANES), F32),
            pltpu.VMEM((NZ - 1, TILES, ROWS + 8, LANES), I32),
            pltpu.VMEM((NZ - 1, TILES, ROWS + 8, LANES), I32),
            pltpu.VMEM((TILES, ROWS, 2 * LANES), F32),
            pltpu.VMEM((2 * ROWS, NLAT), F32),
            pltpu.VMEM((NY, NW, OWN + 8, LANES), I32),
            dma((TILES,)),
            dma((2, TILES, NY)),
            dma((3,)),
            dma((NY + 6,)),
            dma((NY + 6,)),
            dma((2, NZ)),
            dma,
            dma((3, 2, TILES)),
            dma((3, 2, TILES)),
            dma((TILES,)),
            dma((TILES,)),
            dma((NZ - 1, TILES)),
            dma((NZ - 1, TILES)),
            dma((NY, NW)),
            dma((NY, NW)),
            pltpu.SemaphoreType.REGULAR((MEETINGS,)),
        ],
        compiler_params=pltpu.CompilerParams(
            collective_id=0, has_side_effects=True, vmem_limit_bytes=60 * 1024 * 1024
        ),
        name="exchange",
    )(spectral_state, inverse, term_weights, legendre)


def place_kernel(column_ref, code_ref, out_hbm, decoded, sem):
    def out_copy(slot):
        return pltpu.make_async_copy(decoded.at[slot], out_hbm.at[column_ref[slot]], sem.at[slot])

    @pl.loop(0, NW)
    def _(from_w):
        for from_y in range(NY):
            slot = from_w * NY + from_y
            last = code_ref[from_y, from_w, OWN:, :]
            moved = pltpu.roll(last, LANES - 32, 1)
            for part, rest in ((0, last), (1, moved)):
                step = span_of(rest[:, 64:65]) * (1.0 / TOP)
                main = code_ref[from_y, from_w, part * 8 : part * 8 + 8, :]
                wide = jnp.broadcast_to(step, (8, LANES))
                rows = slice(part * 8, part * 8 + 8)
                for p, value in enumerate(unpacked(main, wide)):
                    decoded[slot, p, rows, :LANES] = value
                for p, value in enumerate(unpacked(rest, wide)):
                    decoded[slot, p, rows, LANES:] = value[:, :32]
            out_copy(slot).start()

    @pl.loop(0, NW * NY)
    def _(slot):
        out_copy(slot).wait()


def place(slot_column, codes):
    shape = (NW * NY, 2, OWN, BAND)
    return pl.pallas_call(
        place_kernel,
        out_shape=jax.ShapeDtypeStruct(shape, F32),
        in_specs=[pl.BlockSpec(memory_space=pltpu.SMEM), pl.BlockSpec(memory_space=pltpu.VMEM)],
        out_specs=pl.BlockSpec(memory_space=pl.ANY),
        scratch_shapes=[pltpu.VMEM(shape, F32), pltpu.SemaphoreType.DMA((NW * NY,))],
        compiler_params=pltpu.CompilerParams(vmem_limit_bytes=60 * 1024 * 1024),
        name="place",
    )(slot_column, codes)


def shards(spectral_state, inverse, term_weights, legendre, slot_column):
    codes = exchange(spectral_state, inverse, term_weights, legendre)
    return place(slot_column, codes)


def solution(mesh):
    placed = (
        P("wave", "term", None),
        P("term", "wave", None, None, None),
        P("term", None),
        P("wave", None, None),
        P(),
    )
    return jax.shard_map(
        shards, mesh=mesh, in_specs=placed, out_specs=P(None, None, "term", "wave"), check_vma=False
    )
```

```python
import functools

import jax
import jax.numpy as jnp
from jax import lax
from jax.experimental import pallas as pl
from jax.experimental.pallas import tpu as pltpu
from jax.sharding import PartitionSpec as P

F32 = jnp.float32
BF16 = jnp.bfloat16
I32 = jnp.int32
MESH = pl.DeviceIdType.MESH

NY, NZ, NC, NW = 4, 4, 2, 8
NDEG, NLAT = 640, 1280
OWN = 16
HALF = NDEG // NC
QUARTER = HALF // 2
LANES = 128
TILES = NDEG // LANES
WINDOW = 384
STEPS = 8.0
TOP = 32700.0
BAND = NLAT // NW
ROWS = NY * OWN
CHUNK = 32
MEETINGS = 6


def code_of(height):
    return jnp.ceil(jnp.log2(jnp.maximum(height, 1e-30)) * STEPS).astype(I32)


def span_of(code):
    return jnp.exp2(code.astype(F32) * (1.0 / STEPS))


def gain_of(code):
    return TOP * jnp.exp2(code.astype(F32) * (-1.0 / STEPS))


def packed(real, imag, gain):
    high = (real * gain + 32768.5).astype(I32)
    low = (imag * gain + 32768.5).astype(I32)
    return lax.shift_left(high, jnp.full_like(high, 16)) | low


def unpacked(code, step):
    high = lax.shift_right_logical(code, jnp.full_like(code, 16)).astype(F32)
    low = (code & 0xFFFF).astype(F32)
    return (high - 32768.0) * step, (low - 32768.0) * step


def exchange_kernel(
    x_hbm, inv_hbm, w_hbm, leg_hbm, out_ref,
    raw_own, raw_pal, w_ref, w_pal, x_all, leg, snd, rcv, snd_sum, rcv_sum, work, rhs,
    t_own, t_snd, t_rcv, z_snd, z_rcv, t_fin, grid, pieces,
    raw_own_sem, raw_snd_sem, raw_pal_sem, w_sem, x_snd_sem, x_rcv_sem, x_fwd_sem, leg_sem,
    snd_sem, rcv_sem, t_snd_sem, t_rcv_sem, z_snd_sem, z_rcv_sem, f_snd_sem, f_rcv_sem, met,
):
    term = lax.axis_index("term")
    wave = lax.axis_index("wave")
    core = lax.rem(term, 2)
    y = lax.rem(term // 2, NY)
    z = term // (2 * NY)
    zy = z * NY + y

    def at(z_, y_, core_, wave_):
        return ((z_ * NY + y_) * 2 + core_, wave_)

    pal = at(z, y, 1 - core, wave)

    def own_copy(j):
        return pltpu.make_async_copy(
            inv_hbm.at[0, :, :, pl.ds(pl.multiple_of(core * HALF, 64), HALF), pl.ds(pl.multiple_of(j * LANES, LANES), LANES)],
            raw_own.at[j],
            raw_own_sem.at[j],
        )

    def pal_copy(j, d):
        slot = lax.rem(y + d, NY)
        return pltpu.make_async_remote_copy(
            src_ref=inv_hbm.at[0, slot, :, pl.ds(pl.multiple_of((1 - core) * HALF, 64), HALF), pl.ds(pl.multiple_of(j * LANES, LANES), LANES)],
            dst_ref=raw_pal.at[j, slot],
            send_sem=raw_snd_sem,
            recv_sem=raw_pal_sem.at[j, d],
            device_id=pal,
            device_id_type=MESH,
        )

    w_local = pltpu.make_async_copy(w_hbm, w_ref, w_sem.at[2])
    w_copy = pltpu.make_async_remote_copy(
        src_ref=w_hbm, dst_ref=w_pal, send_sem=w_sem.at[0], recv_sem=w_sem.at[1], device_id=pal, device_id_type=MESH
    )

    def x_part(z_, y_, size):
        return x_all.at[core, pl.ds(pl.multiple_of((z_ * NY + y_) * OWN, OWN), size)]

    def x_copy(dy, source):
        to_y = lax.rem(y + dy, NY)
        return pltpu.make_async_remote_copy(
            src_ref=x_hbm.at[to_y],
            dst_ref=x_part(z, source, OWN),
            send_sem=x_snd_sem.at[dy],
            recv_sem=x_rcv_sem.at[dy],
            device_id=at(z, to_y, core, wave),
            device_id_type=MESH,
        )

    def x_arrival(dy):
        return x_copy(dy, lax.rem(y + NY - dy, NY))

    def x_line_copy(way, hop):
        owner = z + (-hop if way == 0 else hop)
        to_z = z + (1 if way == 0 else -1)
        copy = pltpu.make_async_remote_copy(
            src_ref=x_part(owner, 0, ROWS),
            dst_ref=x_part(owner, 0, ROWS),
            send_sem=x_snd_sem.at[NY + 3 * way + hop],
            recv_sem=x_rcv_sem.at[NY + 3 * way + hop],
            device_id=at(to_z, y, core, wave),
            device_id_type=MESH,
        )
        inside = (owner >= 0) & (to_z < NZ) if way == 0 else (owner < NZ) & (to_z >= 0)
        return copy, inside

    def x_line_arrival(way, hop):
        owner = z + (-1 - hop if way == 0 else 1 + hop)
        copy = pltpu.make_async_remote_copy(
            src_ref=x_part(owner, 0, ROWS),
            dst_ref=x_part(owner, 0, ROWS),
            send_sem=x_snd_sem.at[NY + 3 * way + hop],
            recv_sem=x_rcv_sem.at[NY + 3 * way + hop],
            device_id=pal,
            device_id_type=MESH,
        )
        return copy, owner, (owner >= 0) if way == 0 else (owner < NZ)

    def x_pass(owner, owner_core):
        part = x_all.at[owner_core, pl.ds(pl.multiple_of(owner * ROWS, ROWS), ROWS)]
        return pltpu.make_async_remote_copy(
            src_ref=part,
            dst_ref=part,
            send_sem=x_fwd_sem.at[0, owner],
            recv_sem=x_fwd_sem.at[1, owner],
            device_id=pal,
            device_id_type=MESH,
        )

    def x_line_send(hop):
        for way in range(2):
            copy, inside = x_line_copy(way, hop)
            pl.when(inside)(copy.start)

    def x_line_take(hop):
        for way in range(2):
            copy, owner, present = x_line_arrival(way, hop)

            @pl.when(present)
            def _():
                copy.wait_recv()
                x_pass(owner, core).start()

    x_local = pltpu.make_async_copy(x_hbm.at[y], x_part(z, y, OWN), x_rcv_sem.at[0])
    leg_copy = pltpu.make_async_copy(leg_hbm.at[y], leg, leg_sem)

    def y_copy(kind, way, j):
        to = lax.rem(y + (1 if way == 0 else NY - 1), NY)
        return pltpu.make_async_remote_copy(
            src_ref=(snd, snd_sum)[kind].at[way, j],
            dst_ref=(rcv, rcv_sum)[kind].at[way, j],
            send_sem=snd_sem.at[kind],
            recv_sem=rcv_sem.at[kind, way, j],
            device_id=at(z, to, core, wave),
            device_id_type=MESH,
        )

    def t_copy(j):
        return pltpu.make_async_remote_copy(
            src_ref=t_snd.at[j],
            dst_ref=t_rcv.at[j],
            send_sem=t_snd_sem,
            recv_sem=t_rcv_sem.at[j],
            device_id=pal,
            device_id_type=MESH,
        )

    def z_copy(i, j):
        return pltpu.make_async_remote_copy(
            src_ref=z_snd.at[j, i],
            dst_ref=z_rcv.at[j, i],
            send_sem=z_snd_sem,
            recv_sem=z_rcv_sem.at[j],
            device_id=at(lax.rem(z + 1 + i, NZ), y, core, wave),
            device_id_type=MESH,
        )

    def shifted(z_, steps):
        return lax.rem(z_ + steps, NZ)

    block = shifted(z, 1 + 2 * core)

    def f_copy(dy, dw):
        to_y = lax.rem(y + dy, NY)
        to_w = lax.rem(wave + dw, NW)
        return pltpu.make_async_remote_copy(
            src_ref=pieces.at[to_y, to_w],
            dst_ref=out_ref.at[y, wave],
            send_sem=f_snd_sem,
            recv_sem=f_rcv_sem,
            device_id=at(block, to_y, core, to_w),
            device_id_type=MESH,
        )

    def whole(source, target, send_sem, recv_sem):
        return pltpu.make_async_remote_copy(
            src_ref=source,
            dst_ref=target,
            send_sem=send_sem,
            recv_sem=recv_sem,
            device_id=pal,
            device_id_type=MESH,
        )

    x_pos = wave // 2
    high = lax.rem(wave, 2) * NZ + z

    def place_of(x_, y_, high_):
        return at(lax.rem(high_, NZ), y_, core, x_ * 2 + high_ // NZ)

    around = [
        place_of(lax.rem(x_pos + 1, 4), y, high),
        place_of(lax.rem(x_pos + 3, 4), y, high),
        place_of(x_pos, lax.rem(y + 1, NY), high),
        place_of(x_pos, lax.rem(y + 3, NY), high),
        place_of(x_pos, y, lax.rem(high + 1, 2 * NZ)),
        place_of(x_pos, y, lax.rem(high + 7, 2 * NZ)),
    ]

    def tell(semaphore):
        for device in around:
            pl.semaphore_signal(semaphore, inc=1, device_id=device, device_id_type=MESH)

    barrier = pltpu.get_barrier_semaphore()
    for device in (pal, at(z, lax.rem(y + 2, NY), core, wave)):
        pl.semaphore_signal(barrier, inc=1, device_id=device, device_id_type=MESH)
    tell(barrier)

    @pl.loop(0, TILES)
    def _(j):
        own_copy(j).start()

    w_local.start()
    x_local.start()
    leg_copy.start()
    for side in range(2):
        for base in (0, WINDOW):
            pad = pl.ds(pl.multiple_of(base + (1 - core) * HALF, 64), WINDOW - HALF)
            rhs[side, pad, :] = jnp.zeros((WINDOW - HALF, 2 * LANES), BF16)
    grid[...] = jnp.zeros_like(grid)

    pl.semaphore_wait(barrier, 2 + len(around))
    w_copy.start()

    @pl.loop(0, TILES)
    def _(j):
        for d in (2, 1, 3, 0):
            pal_copy(j, d).start()

    for dy in (2, 1, 3):
        x_copy(dy, y).start()
    tell(met.at[0])
    w_local.wait()
    w_copy.wait()
    weights = [w_ref[0:1, 0:1], w_ref[0:1, 1:2], w_pal[0:1, 0:1], w_pal[0:1, 1:2]]
    weights = [jnp.broadcast_to(v, (CHUNK, LANES)) for v in weights]

    def term_sum(j, slot, row):
        rows = pl.ds(row, CHUNK)
        r0 = raw_own[j, slot, 0, rows, :].astype(F32)
        j0 = raw_own[j, slot, 1, rows, :].astype(F32)
        r1 = raw_pal[j, slot, 0, rows, :].astype(F32)
        j1 = raw_pal[j, slot, 1, rows, :].astype(F32)
        a0, b0, a1, b1 = weights
        return (a0 * r0 - b0 * j0) + (a1 * r1 - b1 * j1), (a0 * j0 + b0 * r0) + (a1 * j1 + b1 * r1)

    def higher(height, real, imag):
        tall = jnp.maximum(jnp.abs(real), jnp.abs(imag))
        return jnp.maximum(height, jnp.max(tall.reshape(-1, 8, LANES), axis=0))

    def step_of(message, rows, size):
        step = span_of(message[rows : rows + 8, :])[0:1] * (1.0 / TOP)
        return jnp.broadcast_to(step, (size, LANES))

    def write_message(to, j, slot, halves, since):
        height = jnp.zeros((8, LANES), F32)
        for place, half in enumerate(halves):
            for part in range(QUARTER // CHUNK):
                base = part * CHUNK
                rows = slice(base, base + CHUNK)
                real, imag = term_sum(j, slot, half * QUARTER + base)
                if since is not None and place == 0:
                    more_real, more_imag = unpacked(since[rows, :], step_of(since, QUARTER, CHUNK))
                    real, imag = real + more_real, imag + more_imag
                rows = slice(place * QUARTER + base, place * QUARTER + base + CHUNK)
                work[0, rows, :] = real
                work[1, rows, :] = imag
                height = higher(height, real, imag)
        height = jnp.broadcast_to(jnp.max(height, axis=0, keepdims=True), (8, LANES))
        code = code_of(height)
        gain = jnp.broadcast_to(gain_of(code)[0:1], (CHUNK, LANES))
        total = QUARTER * len(halves)
        for part in range(total // CHUNK):
            rows = slice(part * CHUNK, (part + 1) * CHUNK)
            to[rows, :] = packed(work[0, rows, :], work[1, rows, :], gain)
        to[total : total + 8, :] = code

    def stage_first(j):
        own_copy(j).wait()
        pal_copy(j, 2).wait_recv()
        for way in range(2):
            write_message(snd.at[way, j], j, lax.rem(y + 2, NY), (way,), None)
            y_copy(0, way, j).start()

    def stage_sum(j):
        for way in range(2):
            d = 1 if way == 0 else NY - 1
            pal_copy(j, d).wait_recv()
            y_copy(0, way, j).wait_recv()
            write_message(snd_sum.at[way, j], j, lax.rem(y + d, NY), (way, 1 - way), rcv.at[way, j])
            y_copy(1, way, j).start()

    def stage_product(j):
        pal_copy(j, 0).wait_recv()
        for way in range(2):
            y_copy(1, way, j).wait_recv()
        steps = [step_of(rcv_sum.at[way, j], HALF, CHUNK) for way in range(2)]
        for half in range(2):
            for part in range(QUARTER // CHUNK):
                start = half * QUARTER + part * CHUNK
                real, imag = term_sum(j, y, start)
                for way in range(2):
                    at_row = part * CHUNK + (0 if way == half else QUARTER)
                    more_real, more_imag = unpacked(
                        rcv_sum[way, j, at_row : at_row + CHUNK, :], steps[way]
                    )
                    real, imag = real + more_real, imag + more_imag
                real_high = real.astype(BF16)
                imag_high = imag.astype(BF16)
                real_low = (real - real_high.astype(F32)).astype(BF16)
                imag_low = (imag - imag_high.astype(F32)).astype(BF16)
                into = pl.ds(pl.multiple_of(core * (WINDOW - HALF) + start, CHUNK), CHUNK)
                also = pl.ds(pl.multiple_of(WINDOW + core * (WINDOW - HALF) + start, CHUNK), CHUNK)
                rhs[0, into, :] = jnp.concatenate([real_high, imag_high], axis=1)
                rhs[1, into, :] = jnp.concatenate([real_low, imag_low], axis=1)
                rhs[0, also, :] = jnp.concatenate([-imag_high, real_high], axis=1)
                rhs[1, also, :] = jnp.concatenate([-imag_low, real_low], axis=1)

        def product(owner):
            left = x_all[owner, :, pl.ds(pl.multiple_of(core * 256, LANES), WINDOW)]
            right = x_all[owner, :, pl.ds(pl.multiple_of(NDEG + core * 256, LANES), WINDOW)]
            both = jnp.concatenate([left, right], axis=1)
            value = jnp.dot(both, rhs[0], preferred_element_type=F32)
            return value + jnp.dot(both, rhs[1], preferred_element_type=F32)

        t_snd[j] = product(1 - core)
        t_copy(j).start()
        t_own[j] = product(core)

    def stage_spread(j):
        t_copy(j).wait_recv()
        for i in range(NZ):
            to = lax.rem(z + 1 + i, NZ)
            rows = pl.ds(pl.multiple_of(shifted(to, 1 + 2 * core) * ROWS, ROWS), ROWS)
            value = t_own[j, rows, :] + t_rcv[j, rows, :]
            if i == NZ - 1:
                t_fin[j] = value
                continue
            real, imag = value[:, :LANES], value[:, LANES:]
            height = higher(jnp.zeros((8, LANES), F32), real, imag)
            height = jnp.broadcast_to(jnp.max(height, axis=0, keepdims=True), (8, LANES))
            code = code_of(height)
            gain = jnp.broadcast_to(gain_of(code)[0:1], (ROWS, LANES))
            z_snd[j, i, :ROWS, :] = packed(real, imag, gain)
            z_snd[j, i, ROWS:, :] = code
            z_copy(i, j).start()

    def stage_synthesis(j):
        whole(z_snd.at[j], z_rcv.at[j], z_snd_sem, z_rcv_sem.at[j]).wait_recv()
        value = t_fin[j]
        real, imag = value[:, :LANES], value[:, LANES:]
        for i in range(NZ - 1):
            step = span_of(z_rcv[j, i, ROWS:, :])[0:1] * (1.0 / TOP)
            step = jnp.broadcast_to(step, (ROWS, LANES))
            more_real, more_imag = unpacked(z_rcv[j, i, :ROWS, :], step)
            real, imag = real + more_real, imag + more_imag
        both = jnp.concatenate([real, imag], axis=0)
        high = both.astype(BF16)
        low = (both - high.astype(F32)).astype(BF16)
        left = jnp.concatenate([high, low], axis=1)
        table = pl.ds(pl.multiple_of(j * LANES, LANES), LANES)

        @pl.loop(0, NLAT // 256)
        def _(i):
            columns = pl.ds(pl.multiple_of(i * 256, 256), 256)
            part = leg[table, columns]
            right = jnp.concatenate([part, part], axis=0)
            grid[:, columns] += jnp.dot(left, right, preferred_element_type=F32)

    @pl.loop(0, 2)
    def _(j):
        stage_first(j)

    x_local.wait()
    for dy in range(1, NY):
        x_arrival(dy).wait_recv()
    x_line_send(0)
    x_pass(z, core).start()

    @pl.loop(0, TILES)
    def _(it):
        stage_sum(it)

        @pl.when(it < TILES - 2)
        def _():
            stage_first(it + 2)

        pl.semaphore_wait(met.at[it], len(around))
        tell(met.at[it + 1])

        @pl.when(it == 0)
        def _():
            x_line_take(0)
            x_line_send(1)

        @pl.when(it == 1)
        def _():
            x_line_take(1)
            x_line_send(2)

        @pl.when(it == 2)
        def _():
            x_line_take(2)
            for owner in range(NZ):
                x_pass(owner, 1 - core).wait_recv()

        @pl.when(it > 2)
        def _():
            @pl.loop(jnp.where(it == 3, 0, 2), jnp.where(it == 3, 2, 3))
            def _(j):
                stage_spread(j)

        @pl.when(it > 1)
        def _():
            @pl.loop(jnp.where(it == 2, 0, it - 1), jnp.where(it == 4, TILES, it))
            def _(j):
                stage_product(j)

                @pl.when(it == 4)
                def _():
                    stage_spread(j)

    leg_copy.wait()
    pl.semaphore_wait(met.at[MEETINGS - 1], len(around))

    @pl.loop(0, TILES)
    def _(j):
        stage_synthesis(j)

    lane = lax.broadcasted_iota(I32, (8, LANES), 1)
    @pl.loop(0, NY)
    def _(turn):
        dy = jnp.where(turn < 3, jnp.where(turn < 1, 2, turn * 2 - 1), 0)
        to_y = lax.rem(y + dy, NY)
        real = grid[pl.ds(pl.multiple_of(to_y * OWN, OWN), OWN), :]
        imag = grid[pl.ds(pl.multiple_of(ROWS + to_y * OWN, OWN), OWN), :]
        height = jnp.max(jnp.maximum(jnp.abs(real), jnp.abs(imag)), axis=1, keepdims=True)
        code = code_of(jnp.broadcast_to(height, (OWN, LANES)))
        gain = gain_of(code)
        gain = jnp.concatenate([gain] * (NLAT // LANES), axis=1)
        value = packed(real, imag, gain)
        for to_w in range(NW):
            tile, skip = divmod(to_w * BAND, LANES)
            band = value[:, tile * LANES : tile * LANES + 2 * LANES]
            if skip:
                band = pltpu.roll(band, 2 * LANES - skip, 1)
            rest = band[:, LANES:]
            last = jnp.where(lane < 96, code[:8], code[8:])
            last = jnp.where(lane < 64, pltpu.roll(rest[8:], 32, 1), last)
            last = jnp.where(lane < 32, rest[:8], last)
            pieces[to_y, to_w, :OWN, :] = band[:, :LANES]
            pieces[to_y, to_w, OWN:, :] = last

        for dw in (5, 3, 1, 7, 4, 2, 6, 0):
            f_copy(dy, dw).start()


    whole(raw_pal, raw_pal, raw_snd_sem, raw_snd_sem).wait_send()
    whole(snd, rcv, snd_sem.at[0], snd_sem.at[0]).wait_send()
    whole(snd_sum, rcv_sum, snd_sem.at[1], snd_sem.at[1]).wait_send()
    whole(t_snd, t_rcv, t_snd_sem, t_snd_sem).wait_send()
    whole(z_snd, z_rcv, z_snd_sem, z_snd_sem).wait_send()
    for d in range(1, NY):
        x_copy(d, y).wait_send()
    for hop in range(3):
        for way in range(2):
            copy, inside = x_line_copy(way, hop)
            pl.when(inside)(copy.wait_send)
    for owner in range(NZ):
        x_pass(owner, core).wait_send()

    whole(pieces, out_ref, f_snd_sem, f_rcv_sem).wait()


def exchange(spectral_state, inverse, term_weights, legendre):
    any_space = pl.BlockSpec(memory_space=pl.ANY)
    dma = pltpu.SemaphoreType.DMA
    return pl.pallas_call(
        exchange_kernel,
        out_shape=jax.ShapeDtypeStruct((NY, NW, OWN + 8, LANES), I32),
        in_specs=[any_space] * 4,
        out_specs=any_space,
        scratch_shapes=[
            pltpu.VMEM((TILES, NY, 2, HALF, LANES), BF16),
            pltpu.VMEM((TILES, NY, 2, HALF, LANES), BF16),
            pltpu.VMEM((1, 2), F32),
            pltpu.VMEM((1, 2), F32),
            pltpu.VMEM((2, NZ * NY * OWN, 2 * NDEG), BF16),
            pltpu.VMEM((NDEG, NLAT), BF16),
            pltpu.VMEM((2, TILES, QUARTER + 8, LANES), I32),
            pltpu.VMEM((2, TILES, QUARTER + 8, LANES), I32),
            pltpu.VMEM((2, TILES, HALF + 8, LANES), I32),
            pltpu.VMEM((2, TILES, HALF + 8, LANES), I32),
            pltpu.VMEM((2, HALF, LANES), F32),
            pltpu.VMEM((2, 2 * WINDOW, 2 * LANES), BF16),
            pltpu.VMEM((TILES, 256, 2 * LANES), F32),
            pltpu.VMEM((TILES, 256, 2 * LANES), F32),
            pltpu.VMEM((TILES, 256, 2 * LANES), F32),
            pltpu.VMEM((TILES, NZ - 1, ROWS + 8, LANES), I32),
            pltpu.VMEM((TILES, NZ - 1, ROWS + 8, LANES), I32),
            pltpu.VMEM((TILES, ROWS, 2 * LANES), F32),
            pltpu.VMEM((2 * ROWS, NLAT), F32),
            pltpu.VMEM((NY, NW, OWN + 8, LANES), I32),
            dma((TILES,)),
            dma,
            dma((TILES, NY)),
            dma((3,)),
            dma((NY + 6,)),
            dma((NY + 6,)),
            dma((2, NZ)),
            dma,
            dma((2,)),
            dma((2, 2, TILES)),
            dma,
            dma((TILES,)),
            dma,
            dma((TILES,)),
            dma,
            dma,
            pltpu.SemaphoreType.REGULAR((MEETINGS,)),
        ],
        compiler_params=pltpu.CompilerParams(
            collective_id=0, has_side_effects=True, vmem_limit_bytes=60 * 1024 * 1024
        ),
        name="exchange",
    )(spectral_state, inverse, term_weights, legendre)


def place_kernel(column_ref, code_ref, out_hbm, decoded, sem):
    def out_copy(slot):
        return pltpu.make_async_copy(decoded.at[slot], out_hbm.at[column_ref[slot]], sem.at[slot])

    @pl.loop(0, NW // 4)
    def _(group):
        for index in range(4 * NY):
            from_w = group * 4 + index // NY
            from_y = index % NY
            slot = from_w * NY + from_y
            last = code_ref[from_y, from_w, OWN:, :]
            moved = pltpu.roll(last, LANES - 32, 1)
            for part, rest in ((0, last), (1, moved)):
                step = span_of(rest[:, 64:65]) * (1.0 / TOP)
                main = code_ref[from_y, from_w, part * 8 : part * 8 + 8, :]
                wide = jnp.broadcast_to(step, (8, LANES))
                rows = slice(part * 8, part * 8 + 8)
                for p, value in enumerate(unpacked(main, wide)):
                    decoded[slot, p, rows, :LANES] = value
                for p, value in enumerate(unpacked(rest, wide)):
                    decoded[slot, p, rows, LANES:] = value[:, :32]
            out_copy(slot).start()

    @pl.loop(0, NW * NY)
    def _(slot):
        out_copy(slot).wait()


def place(slot_column, codes):
    shape = (NW * NY, 2, OWN, BAND)
    return pl.pallas_call(
        place_kernel,
        out_shape=jax.ShapeDtypeStruct(shape, F32),
        in_specs=[pl.BlockSpec(memory_space=pltpu.SMEM), pl.BlockSpec(memory_space=pltpu.VMEM)],
        out_specs=pl.BlockSpec(memory_space=pl.ANY),
        scratch_shapes=[pltpu.VMEM(shape, F32), pltpu.SemaphoreType.DMA((NW * NY,))],
        compiler_params=pltpu.CompilerParams(vmem_limit_bytes=60 * 1024 * 1024),
        name="place",
    )(slot_column, codes)


def shards(spectral_state, inverse, term_weights, legendre, slot_column):
    codes = exchange(spectral_state, inverse, term_weights, legendre)
    return place(slot_column, codes)


def solution(mesh):
    placed = (
        P("wave", "term", None),
        P("term", "wave", None, None, None),
        P("term", None),
        P("wave", None, None),
        P(),
    )
    return jax.shard_map(
        shards, mesh=mesh, in_specs=placed, out_specs=P(None, None, "term", "wave"), check_vma=False
    )
```

```python
import functools

import jax
import jax.numpy as jnp
from jax import lax
from jax.experimental import pallas as pl
from jax.experimental.pallas import tpu as pltpu
from jax.sharding import PartitionSpec as P

F32 = jnp.float32
BF16 = jnp.bfloat16
I32 = jnp.int32
MESH = pl.DeviceIdType.MESH

NY, NZ, NC, NW = 4, 4, 2, 8
NDEG, NLAT = 640, 1280
OWN = 16
HALF = NDEG // NC
QUARTER = HALF // 2
LANES = 128
TILES = NDEG // LANES
WINDOW = 384
STEPS = 8.0
TOP = 32700.0
BAND = NLAT // NW
ROWS = NY * OWN
CHUNK = 32
MEETINGS = 6


def code_of(height):
    return jnp.ceil(jnp.log2(jnp.maximum(height, 1e-30)) * STEPS).astype(I32)


def span_of(code):
    return jnp.exp2(code.astype(F32) * (1.0 / STEPS))


def gain_of(code):
    return TOP * jnp.exp2(code.astype(F32) * (-1.0 / STEPS))


def packed(real, imag, gain):
    high = (real * gain + 32768.5).astype(I32)
    low = (imag * gain + 32768.5).astype(I32)
    return lax.shift_left(high, jnp.full_like(high, 16)) | low


def unpacked(code, step):
    high = lax.shift_right_logical(code, jnp.full_like(code, 16)).astype(F32)
    low = (code & 0xFFFF).astype(F32)
    return (high - 32768.0) * step, (low - 32768.0) * step


def exchange_kernel(
    x_hbm, inv_hbm, w_hbm, leg_hbm, out_ref,
    raw_own, raw_pal, w_ref, w_pal, x_all, leg, snd, rcv, snd_sum, rcv_sum, work, rhs,
    t_own, t_snd, t_rcv, z_snd, z_rcv, t_fin, grid, pieces,
    raw_own_sem, raw_snd_sem, raw_pal_sem, w_sem, x_snd_sem, x_rcv_sem, x_fwd_sem, leg_sem,
    snd_sem, rcv_sem, t_snd_sem, t_rcv_sem, z_snd_sem, z_rcv_sem, f_snd_sem, f_rcv_sem, met,
):
    term = lax.axis_index("term")
    wave = lax.axis_index("wave")
    core = lax.rem(term, 2)
    y = lax.rem(term // 2, NY)
    z = term // (2 * NY)
    zy = z * NY + y

    def at(z_, y_, core_, wave_):
        return ((z_ * NY + y_) * 2 + core_, wave_)

    pal = at(z, y, 1 - core, wave)

    def own_copy(j):
        return pltpu.make_async_copy(
            inv_hbm.at[0, :, :, pl.ds(pl.multiple_of(core * HALF, 64), HALF), pl.ds(pl.multiple_of(j * LANES, LANES), LANES)],
            raw_own.at[j],
            raw_own_sem.at[j],
        )

    def pal_copy(j, d):
        slot = lax.rem(y + d, NY)
        return pltpu.make_async_remote_copy(
            src_ref=inv_hbm.at[0, slot, :, pl.ds(pl.multiple_of((1 - core) * HALF, 64), HALF), pl.ds(pl.multiple_of(j * LANES, LANES), LANES)],
            dst_ref=raw_pal.at[j, slot],
            send_sem=raw_snd_sem,
            recv_sem=raw_pal_sem.at[j, d],
            device_id=pal,
            device_id_type=MESH,
        )

    w_local = pltpu.make_async_copy(w_hbm, w_ref, w_sem.at[2])
    w_copy = pltpu.make_async_remote_copy(
        src_ref=w_hbm, dst_ref=w_pal, send_sem=w_sem.at[0], recv_sem=w_sem.at[1], device_id=pal, device_id_type=MESH
    )

    def x_part(z_, y_, size):
        return x_all.at[core, pl.ds(pl.multiple_of((z_ * NY + y_) * OWN, OWN), size)]

    def x_copy(dy, source):
        to_y = lax.rem(y + dy, NY)
        return pltpu.make_async_remote_copy(
            src_ref=x_hbm.at[to_y],
            dst_ref=x_part(z, source, OWN),
            send_sem=x_snd_sem.at[dy],
            recv_sem=x_rcv_sem.at[dy],
            device_id=at(z, to_y, core, wave),
            device_id_type=MESH,
        )

    def x_arrival(dy):
        return x_copy(dy, lax.rem(y + NY - dy, NY))

    def x_line_copy(way, hop):
        owner = z + (-hop if way == 0 else hop)
        to_z = z + (1 if way == 0 else -1)
        copy = pltpu.make_async_remote_copy(
            src_ref=x_part(owner, 0, ROWS),
            dst_ref=x_part(owner, 0, ROWS),
            send_sem=x_snd_sem.at[NY + 3 * way + hop],
            recv_sem=x_rcv_sem.at[NY + 3 * way + hop],
            device_id=at(to_z, y, core, wave),
            device_id_type=MESH,
        )
        inside = (owner >= 0) & (to_z < NZ) if way == 0 else (owner < NZ) & (to_z >= 0)
        return copy, inside

    def x_line_arrival(way, hop):
        owner = z + (-1 - hop if way == 0 else 1 + hop)
        copy = pltpu.make_async_remote_copy(
            src_ref=x_part(owner, 0, ROWS),
            dst_ref=x_part(owner, 0, ROWS),
            send_sem=x_snd_sem.at[NY + 3 * way + hop],
            recv_sem=x_rcv_sem.at[NY + 3 * way + hop],
            device_id=pal,
            device_id_type=MESH,
        )
        return copy, owner, (owner >= 0) if way == 0 else (owner < NZ)

    def x_pass(owner, owner_core):
        part = x_all.at[owner_core, pl.ds(pl.multiple_of(owner * ROWS, ROWS), ROWS)]
        return pltpu.make_async_remote_copy(
            src_ref=part,
            dst_ref=part,
            send_sem=x_fwd_sem.at[0, owner],
            recv_sem=x_fwd_sem.at[1, owner],
            device_id=pal,
            device_id_type=MESH,
        )

    def x_line_send(hop):
        for way in range(2):
            copy, inside = x_line_copy(way, hop)
            pl.when(inside)(copy.start)

    def x_line_take(hop):
        for way in range(2):
            copy, owner, present = x_line_arrival(way, hop)

            @pl.when(present)
            def _():
                copy.wait_recv()
                x_pass(owner, core).start()

    x_local = pltpu.make_async_copy(x_hbm.at[y], x_part(z, y, OWN), x_rcv_sem.at[0])
    leg_copy = pltpu.make_async_copy(leg_hbm.at[y], leg, leg_sem)

    def y_copy(kind, way, j):
        to = lax.rem(y + (1 if way == 0 else NY - 1), NY)
        return pltpu.make_async_remote_copy(
            src_ref=(snd, snd_sum)[kind].at[way, j],
            dst_ref=(rcv, rcv_sum)[kind].at[way, j],
            send_sem=snd_sem.at[kind],
            recv_sem=rcv_sem.at[kind, way, j],
            device_id=at(z, to, core, wave),
            device_id_type=MESH,
        )

    def t_copy(j):
        return pltpu.make_async_remote_copy(
            src_ref=t_snd.at[j],
            dst_ref=t_rcv.at[j],
            send_sem=t_snd_sem,
            recv_sem=t_rcv_sem.at[j],
            device_id=pal,
            device_id_type=MESH,
        )

    def z_copy(i, j):
        return pltpu.make_async_remote_copy(
            src_ref=z_snd.at[j, i],
            dst_ref=z_rcv.at[j, i],
            send_sem=z_snd_sem,
            recv_sem=z_rcv_sem.at[j],
            device_id=at(lax.rem(z + 1 + i, NZ), y, core, wave),
            device_id_type=MESH,
        )

    def shifted(z_, steps):
        return lax.rem(z_ + steps, NZ)

    block = shifted(z, NZ // 2)

    def f_copy(dy, dw):
        to_y = lax.rem(y + dy, NY)
        to_w = lax.rem(wave + dw, NW)
        return pltpu.make_async_remote_copy(
            src_ref=pieces.at[to_y, to_w],
            dst_ref=out_ref.at[y, wave],
            send_sem=f_snd_sem,
            recv_sem=f_rcv_sem,
            device_id=at(block, to_y, core, to_w),
            device_id_type=MESH,
        )

    def whole(source, target, send_sem, recv_sem):
        return pltpu.make_async_remote_copy(
            src_ref=source,
            dst_ref=target,
            send_sem=send_sem,
            recv_sem=recv_sem,
            device_id=pal,
            device_id_type=MESH,
        )

    x_pos = wave // 2
    high = lax.rem(wave, 2) * NZ + z

    def place_of(x_, y_, high_):
        return at(lax.rem(high_, NZ), y_, core, x_ * 2 + high_ // NZ)

    around = [
        place_of(lax.rem(x_pos + 1, 4), y, high),
        place_of(lax.rem(x_pos + 3, 4), y, high),
        place_of(x_pos, lax.rem(y + 1, NY), high),
        place_of(x_pos, lax.rem(y + 3, NY), high),
        place_of(x_pos, y, lax.rem(high + 1, 2 * NZ)),
        place_of(x_pos, y, lax.rem(high + 7, 2 * NZ)),
    ]

    def tell(semaphore):
        for device in around:
            pl.semaphore_signal(semaphore, inc=1, device_id=device, device_id_type=MESH)

    barrier = pltpu.get_barrier_semaphore()
    for device in (pal, at(z, lax.rem(y + 2, NY), core, wave)):
        pl.semaphore_signal(barrier, inc=1, device_id=device, device_id_type=MESH)
    tell(barrier)

    @pl.loop(0, TILES)
    def _(j):
        own_copy(j).start()

    w_local.start()
    x_local.start()
    leg_copy.start()
    for side in range(2):
        for base in (0, WINDOW):
            pad = pl.ds(pl.multiple_of(base + (1 - core) * HALF, 64), WINDOW - HALF)
            rhs[side, pad, :] = jnp.zeros((WINDOW - HALF, 2 * LANES), BF16)
    grid[...] = jnp.zeros_like(grid)

    pl.semaphore_wait(barrier, 2 + len(around))
    w_copy.start()

    @pl.loop(0, TILES)
    def _(j):
        for d in (2, 1, 3, 0):
            pal_copy(j, d).start()

    for dy in (2, 1, 3):
        x_copy(dy, y).start()
    tell(met.at[0])
    w_local.wait()
    w_copy.wait()
    weights = [w_ref[0:1, 0:1], w_ref[0:1, 1:2], w_pal[0:1, 0:1], w_pal[0:1, 1:2]]
    weights = [jnp.broadcast_to(v, (CHUNK, LANES)) for v in weights]

    def term_sum(j, slot, row):
        rows = pl.ds(row, CHUNK)
        r0 = raw_own[j, slot, 0, rows, :].astype(F32)
        j0 = raw_own[j, slot, 1, rows, :].astype(F32)
        r1 = raw_pal[j, slot, 0, rows, :].astype(F32)
        j1 = raw_pal[j, slot, 1, rows, :].astype(F32)
        a0, b0, a1, b1 = weights
        return (a0 * r0 - b0 * j0) + (a1 * r1 - b1 * j1), (a0 * j0 + b0 * r0) + (a1 * j1 + b1 * r1)

    def higher(height, real, imag):
        tall = jnp.maximum(jnp.abs(real), jnp.abs(imag))
        return jnp.maximum(height, jnp.max(tall.reshape(-1, 8, LANES), axis=0))

    def step_of(message, rows, size):
        step = span_of(message[rows : rows + 8, :])[0:1] * (1.0 / TOP)
        return jnp.broadcast_to(step, (size, LANES))

    def write_message(to, j, slot, halves, since):
        height = jnp.zeros((8, LANES), F32)
        for place, half in enumerate(halves):
            for part in range(QUARTER // CHUNK):
                base = part * CHUNK
                rows = slice(base, base + CHUNK)
                real, imag = term_sum(j, slot, half * QUARTER + base)
                if since is not None and place == 0:
                    more_real, more_imag = unpacked(since[rows, :], step_of(since, QUARTER, CHUNK))
                    real, imag = real + more_real, imag + more_imag
                rows = slice(place * QUARTER + base, place * QUARTER + base + CHUNK)
                work[0, rows, :] = real
                work[1, rows, :] = imag
                height = higher(height, real, imag)
        height = jnp.broadcast_to(jnp.max(height, axis=0, keepdims=True), (8, LANES))
        code = code_of(height)
        gain = jnp.broadcast_to(gain_of(code)[0:1], (CHUNK, LANES))
        total = QUARTER * len(halves)
        for part in range(total // CHUNK):
            rows = slice(part * CHUNK, (part + 1) * CHUNK)
            to[rows, :] = packed(work[0, rows, :], work[1, rows, :], gain)
        to[total : total + 8, :] = code

    def stage_first(j):
        own_copy(j).wait()
        pal_copy(j, 2).wait_recv()
        for way in range(2):
            write_message(snd.at[way, j], j, lax.rem(y + 2, NY), (way,), None)
            y_copy(0, way, j).start()

    def stage_sum(j):
        for way in range(2):
            d = 1 if way == 0 else NY - 1
            pal_copy(j, d).wait_recv()
            y_copy(0, way, j).wait_recv()
            write_message(snd_sum.at[way, j], j, lax.rem(y + d, NY), (way, 1 - way), rcv.at[way, j])
            y_copy(1, way, j).start()

    def stage_product(j):
        pal_copy(j, 0).wait_recv()
        for part in range(HALF // CHUNK):
            rows = slice(part * CHUNK, (part + 1) * CHUNK)
            work[0, rows, :], work[1, rows, :] = term_sum(j, y, part * CHUNK)
        for way in range(2):
            y_copy(1, way, j).wait_recv()
        steps = [step_of(rcv_sum.at[way, j], HALF, CHUNK) for way in range(2)]
        for half in range(2):
            for part in range(QUARTER // CHUNK):
                start = half * QUARTER + part * CHUNK
                real = work[0, start : start + CHUNK, :]
                imag = work[1, start : start + CHUNK, :]
                for way in range(2):
                    at_row = part * CHUNK + (0 if way == half else QUARTER)
                    more_real, more_imag = unpacked(
                        rcv_sum[way, j, at_row : at_row + CHUNK, :], steps[way]
                    )
                    real, imag = real + more_real, imag + more_imag
                real_high = real.astype(BF16)
                imag_high = imag.astype(BF16)
                real_low = (real - real_high.astype(F32)).astype(BF16)
                imag_low = (imag - imag_high.astype(F32)).astype(BF16)
                into = pl.ds(pl.multiple_of(core * (WINDOW - HALF) + start, CHUNK), CHUNK)
                also = pl.ds(pl.multiple_of(WINDOW + core * (WINDOW - HALF) + start, CHUNK), CHUNK)
                rhs[0, into, :] = jnp.concatenate([real_high, imag_high], axis=1)
                rhs[1, into, :] = jnp.concatenate([real_low, imag_low], axis=1)
                rhs[0, also, :] = jnp.concatenate([-imag_high, real_high], axis=1)
                rhs[1, also, :] = jnp.concatenate([-imag_low, real_low], axis=1)

        def product(owner):
            left = x_all[owner, :, pl.ds(pl.multiple_of(core * 256, LANES), WINDOW)]
            right = x_all[owner, :, pl.ds(pl.multiple_of(NDEG + core * 256, LANES), WINDOW)]
            both = jnp.concatenate([left, right], axis=1)
            value = jnp.dot(both, rhs[0], preferred_element_type=F32)
            return value + jnp.dot(both, rhs[1], preferred_element_type=F32)

        t_snd[j] = product(1 - core)
        t_copy(j).start()
        t_own[j] = product(core)

    def stage_spread(j):
        t_copy(j).wait_recv()
        own_rows = pl.ds(pl.multiple_of(block * ROWS, ROWS), ROWS)
        for turn in range(NZ - 1):
            middle = (1, 0, 2)[turn]
            i = jnp.where(z == 0, NZ - 2 - turn, jnp.where(z == NZ - 1, turn, middle))
            rows = pl.ds(pl.multiple_of(shifted(z + 1 + i, NZ // 2) * ROWS, ROWS), ROWS)
            value = t_own[j, rows, :] + t_rcv[j, rows, :]
            real, imag = value[:, :LANES], value[:, LANES:]
            height = higher(jnp.zeros((8, LANES), F32), real, imag)
            height = jnp.broadcast_to(jnp.max(height, axis=0, keepdims=True), (8, LANES))
            code = code_of(height)
            gain = jnp.broadcast_to(gain_of(code)[0:1], (ROWS, LANES))
            z_snd[j, i, :ROWS, :] = packed(real, imag, gain)
            z_snd[j, i, ROWS:, :] = code
            z_copy(i, j).start()
        t_fin[j] = t_own[j, own_rows, :] + t_rcv[j, own_rows, :]

    def stage_synthesis(j):
        whole(z_snd.at[j], z_rcv.at[j], z_snd_sem, z_rcv_sem.at[j]).wait_recv()
        value = t_fin[j]
        real, imag = value[:, :LANES], value[:, LANES:]
        for i in range(NZ - 1):
            step = span_of(z_rcv[j, i, ROWS:, :])[0:1] * (1.0 / TOP)
            step = jnp.broadcast_to(step, (ROWS, LANES))
            more_real, more_imag = unpacked(z_rcv[j, i, :ROWS, :], step)
            real, imag = real + more_real, imag + more_imag
        both = jnp.concatenate([real, imag], axis=0)
        high = both.astype(BF16)
        low = (both - high.astype(F32)).astype(BF16)
        left = jnp.concatenate([high, low], axis=1)
        table = pl.ds(pl.multiple_of(j * LANES, LANES), LANES)

        @pl.loop(0, NLAT // 256)
        def _(i):
            columns = pl.ds(pl.multiple_of(i * 256, 256), 256)
            part = leg[table, columns]
            right = jnp.concatenate([part, part], axis=0)
            grid[:, columns] += jnp.dot(left, right, preferred_element_type=F32)

    @pl.loop(0, 2)
    def _(j):
        stage_first(j)

    x_local.wait()
    for dy in range(1, NY):
        x_arrival(dy).wait_recv()
    x_line_send(0)
    x_pass(z, core).start()

    @pl.loop(0, TILES)
    def _(it):
        stage_sum(it)

        @pl.when(it < TILES - 2)
        def _():
            stage_first(it + 2)

        pl.semaphore_wait(met.at[it], len(around))
        tell(met.at[it + 1])

        @pl.when(it == 0)
        def _():
            x_line_take(0)
            x_line_send(1)

        @pl.when(it == 1)
        def _():
            x_line_take(1)
            x_line_send(2)

        @pl.when(it == 2)
        def _():
            x_line_take(2)
            for owner in range(NZ):
                x_pass(owner, 1 - core).wait_recv()

        @pl.when(it > 2)
        def _():
            @pl.loop(jnp.where(it == 3, 0, 2), jnp.where(it == 3, 2, 3))
            def _(j):
                stage_spread(j)

        @pl.when(it > 1)
        def _():
            @pl.loop(jnp.where(it == 2, 0, it - 1), jnp.where(it == 4, TILES, it))
            def _(j):
                stage_product(j)

                @pl.when(it == 4)
                def _():
                    stage_spread(j)

    leg_copy.wait()
    pl.semaphore_wait(met.at[MEETINGS - 1], len(around))

    @pl.loop(0, TILES)
    def _(j):
        stage_synthesis(j)

    lane = lax.broadcasted_iota(I32, (8, LANES), 1)
    @pl.loop(0, NY)
    def _(turn):
        dy = jnp.where(turn < 3, jnp.where(turn < 1, 2, turn * 2 - 1), 0)
        to_y = lax.rem(y + dy, NY)
        real = grid[pl.ds(pl.multiple_of(to_y * OWN, OWN), OWN), :]
        imag = grid[pl.ds(pl.multiple_of(ROWS + to_y * OWN, OWN), OWN), :]
        height = jnp.max(jnp.maximum(jnp.abs(real), jnp.abs(imag)), axis=1, keepdims=True)
        code = code_of(jnp.broadcast_to(height, (OWN, LANES)))
        gain = gain_of(code)
        gain = jnp.concatenate([gain] * (NLAT // LANES), axis=1)
        value = packed(real, imag, gain)
        for to_w in range(NW):
            tile, skip = divmod(to_w * BAND, LANES)
            band = value[:, tile * LANES : tile * LANES + 2 * LANES]
            if skip:
                band = pltpu.roll(band, 2 * LANES - skip, 1)
            rest = band[:, LANES:]
            last = jnp.where(lane < 96, code[:8], code[8:])
            last = jnp.where(lane < 64, pltpu.roll(rest[8:], 32, 1), last)
            last = jnp.where(lane < 32, rest[:8], last)
            pieces[to_y, to_w, :OWN, :] = band[:, :LANES]
            pieces[to_y, to_w, OWN:, :] = last

        for dw in (5, 3, 1, 7, 4, 2, 6, 0):
            f_copy(dy, dw).start()


    whole(raw_pal, raw_pal, raw_snd_sem, raw_snd_sem).wait_send()
    whole(snd, rcv, snd_sem.at[0], snd_sem.at[0]).wait_send()
    whole(snd_sum, rcv_sum, snd_sem.at[1], snd_sem.at[1]).wait_send()
    whole(t_snd, t_rcv, t_snd_sem, t_snd_sem).wait_send()
    whole(z_snd, z_rcv, z_snd_sem, z_snd_sem).wait_send()
    for d in range(1, NY):
        x_copy(d, y).wait_send()
    for hop in range(3):
        for way in range(2):
            copy, inside = x_line_copy(way, hop)
            pl.when(inside)(copy.wait_send)
    for owner in range(NZ):
        x_pass(owner, core).wait_send()

    whole(pieces, out_ref, f_snd_sem, f_rcv_sem).wait()


def exchange(spectral_state, inverse, term_weights, legendre):
    any_space = pl.BlockSpec(memory_space=pl.ANY)
    dma = pltpu.SemaphoreType.DMA
    return pl.pallas_call(
        exchange_kernel,
        out_shape=jax.ShapeDtypeStruct((NY, NW, OWN + 8, LANES), I32),
        in_specs=[any_space] * 4,
        out_specs=any_space,
        scratch_shapes=[
            pltpu.VMEM((TILES, NY, 2, HALF, LANES), BF16),
            pltpu.VMEM((TILES, NY, 2, HALF, LANES), BF16),
            pltpu.VMEM((1, 2), F32),
            pltpu.VMEM((1, 2), F32),
            pltpu.VMEM((2, NZ * NY * OWN, 2 * NDEG), BF16),
            pltpu.VMEM((NDEG, NLAT), BF16),
            pltpu.VMEM((2, TILES, QUARTER + 8, LANES), I32),
            pltpu.VMEM((2, TILES, QUARTER + 8, LANES), I32),
            pltpu.VMEM((2, TILES, HALF + 8, LANES), I32),
            pltpu.VMEM((2, TILES, HALF + 8, LANES), I32),
            pltpu.VMEM((2, HALF, LANES), F32),
            pltpu.VMEM((2, 2 * WINDOW, 2 * LANES), BF16),
            pltpu.VMEM((TILES, 256, 2 * LANES), F32),
            pltpu.VMEM((TILES, 256, 2 * LANES), F32),
            pltpu.VMEM((TILES, 256, 2 * LANES), F32),
            pltpu.VMEM((TILES, NZ - 1, ROWS + 8, LANES), I32),
            pltpu.VMEM((TILES, NZ - 1, ROWS + 8, LANES), I32),
            pltpu.VMEM((TILES, ROWS, 2 * LANES), F32),
            pltpu.VMEM((2 * ROWS, NLAT), F32),
            pltpu.VMEM((NY, NW, OWN + 8, LANES), I32),
            dma((TILES,)),
            dma,
            dma((TILES, NY)),
            dma((3,)),
            dma((NY + 6,)),
            dma((NY + 6,)),
            dma((2, NZ)),
            dma,
            dma((2,)),
            dma((2, 2, TILES)),
            dma,
            dma((TILES,)),
            dma,
            dma((TILES,)),
            dma,
            dma,
            pltpu.SemaphoreType.REGULAR((MEETINGS,)),
        ],
        compiler_params=pltpu.CompilerParams(
            collective_id=0, has_side_effects=True, vmem_limit_bytes=60 * 1024 * 1024
        ),
        name="exchange",
    )(spectral_state, inverse, term_weights, legendre)


def place_kernel(column_ref, code_ref, out_hbm, decoded, sem):
    def out_copy(slot):
        return pltpu.make_async_copy(decoded.at[slot], out_hbm.at[column_ref[slot]], sem.at[slot])

    @pl.loop(0, NW // 4)
    def _(group):
        for index in range(4 * NY):
            from_w = group * 4 + index // NY
            from_y = index % NY
            slot = from_w * NY + from_y
            last = code_ref[from_y, from_w, OWN:, :]
            moved = pltpu.roll(last, LANES - 32, 1)
            for part, rest in ((0, last), (1, moved)):
                step = span_of(rest[:, 64:65]) * (1.0 / TOP)
                main = code_ref[from_y, from_w, part * 8 : part * 8 + 8, :]
                wide = jnp.broadcast_to(step, (8, LANES))
                rows = slice(part * 8, part * 8 + 8)
                for p, value in enumerate(unpacked(main, wide)):
                    decoded[slot, p, rows, :LANES] = value
                for p, value in enumerate(unpacked(rest, wide)):
                    decoded[slot, p, rows, LANES:] = value[:, :32]
            out_copy(slot).start()

    @pl.loop(0, NW * NY)
    def _(slot):
        out_copy(slot).wait()


def place(slot_column, codes):
    shape = (NW * NY, 2, OWN, BAND)
    return pl.pallas_call(
        place_kernel,
        out_shape=jax.ShapeDtypeStruct(shape, F32),
        in_specs=[pl.BlockSpec(memory_space=pltpu.SMEM), pl.BlockSpec(memory_space=pltpu.VMEM)],
        out_specs=pl.BlockSpec(memory_space=pl.ANY),
        scratch_shapes=[pltpu.VMEM(shape, F32), pltpu.SemaphoreType.DMA((NW * NY,))],
        compiler_params=pltpu.CompilerParams(vmem_limit_bytes=60 * 1024 * 1024),
        name="place",
    )(slot_column, codes)


def shards(spectral_state, inverse, term_weights, legendre, slot_column):
    codes = exchange(spectral_state, inverse, term_weights, legendre)
    return place(slot_column, codes)


def solution(mesh):
    placed = (
        P("wave", "term", None),
        P("term", "wave", None, None, None),
        P("term", None),
        P("wave", None, None),
        P(),
    )
    return jax.shard_map(
        shards, mesh=mesh, in_specs=placed, out_specs=P(None, None, "term", "wave"), check_vma=False
    )
```

```python
import functools

import jax
import jax.numpy as jnp
from jax import lax
from jax.experimental import pallas as pl
from jax.experimental.pallas import tpu as pltpu
from jax.sharding import PartitionSpec as P

F32 = jnp.float32
BF16 = jnp.bfloat16
I32 = jnp.int32
MESH = pl.DeviceIdType.MESH

NY, NZ, NC, NW = 4, 4, 2, 8
NDEG, NLAT = 640, 1280
OWN = 16
HALF = NDEG // NC
QUARTER = HALF // 2
LANES = 128
TILES = NDEG // LANES
WINDOW = 384
STEPS = 8.0
TOP = 32700.0
BAND = NLAT // NW
ROWS = NY * OWN
CHUNK = 32
MEETINGS = 6


def code_of(height):
    return jnp.ceil(jnp.log2(jnp.maximum(height, 1e-30)) * STEPS).astype(I32)


def span_of(code):
    return jnp.exp2(code.astype(F32) * (1.0 / STEPS))


def gain_of(code):
    return TOP * jnp.exp2(code.astype(F32) * (-1.0 / STEPS))


def packed(real, imag, gain):
    high = (real * gain + 32768.5).astype(I32)
    low = (imag * gain + 32768.5).astype(I32)
    return lax.shift_left(high, jnp.full_like(high, 16)) | low


def unpacked(code, step):
    high = lax.shift_right_logical(code, jnp.full_like(code, 16)).astype(F32)
    low = (code & 0xFFFF).astype(F32)
    return (high - 32768.0) * step, (low - 32768.0) * step


def exchange_kernel(
    x_hbm, inv_hbm, w_hbm, leg_hbm, out_ref,
    raw_own, raw_pal, w_ref, w_pal, x_all, leg, snd, rcv, snd_sum, rcv_sum, work, rhs,
    t_own, t_snd, t_rcv, z_snd, z_rcv, t_fin, grid, pieces,
    raw_own_sem, raw_snd_sem, raw_pal_sem, w_sem, x_snd_sem, x_rcv_sem, x_fwd_sem, leg_sem,
    snd_sem, rcv_sem, t_snd_sem, t_rcv_sem, z_snd_sem, z_rcv_sem, f_snd_sem, f_rcv_sem, met,
):
    term = lax.axis_index("term")
    wave = lax.axis_index("wave")
    core = lax.rem(term, 2)
    y = lax.rem(term // 2, NY)
    z = term // (2 * NY)
    zy = z * NY + y

    def at(z_, y_, core_, wave_):
        return ((z_ * NY + y_) * 2 + core_, wave_)

    pal = at(z, y, 1 - core, wave)

    def own_copy(j):
        return pltpu.make_async_copy(
            inv_hbm.at[0, :, :, pl.ds(pl.multiple_of(core * HALF, 64), HALF), pl.ds(pl.multiple_of(j * LANES, LANES), LANES)],
            raw_own.at[j],
            raw_own_sem.at[j],
        )

    def pal_copy(j, d):
        slot = lax.rem(y + d, NY)
        return pltpu.make_async_remote_copy(
            src_ref=inv_hbm.at[0, slot, :, pl.ds(pl.multiple_of((1 - core) * HALF, 64), HALF), pl.ds(pl.multiple_of(j * LANES, LANES), LANES)],
            dst_ref=raw_pal.at[j, slot],
            send_sem=raw_snd_sem,
            recv_sem=raw_pal_sem.at[j, d],
            device_id=pal,
            device_id_type=MESH,
        )

    w_local = pltpu.make_async_copy(w_hbm, w_ref, w_sem.at[2])
    w_copy = pltpu.make_async_remote_copy(
        src_ref=w_hbm, dst_ref=w_pal, send_sem=w_sem.at[0], recv_sem=w_sem.at[1], device_id=pal, device_id_type=MESH
    )

    def x_part(z_, y_, size):
        return x_all.at[core, pl.ds(pl.multiple_of((z_ * NY + y_) * OWN, OWN), size)]

    def x_copy(dy, source):
        to_y = lax.rem(y + dy, NY)
        return pltpu.make_async_remote_copy(
            src_ref=x_hbm.at[to_y],
            dst_ref=x_part(z, source, OWN),
            send_sem=x_snd_sem.at[dy],
            recv_sem=x_rcv_sem.at[dy],
            device_id=at(z, to_y, core, wave),
            device_id_type=MESH,
        )

    def x_arrival(dy):
        return x_copy(dy, lax.rem(y + NY - dy, NY))

    def x_line_copy(way, hop):
        owner = z + (-hop if way == 0 else hop)
        to_z = z + (1 if way == 0 else -1)
        copy = pltpu.make_async_remote_copy(
            src_ref=x_part(owner, 0, ROWS),
            dst_ref=x_part(owner, 0, ROWS),
            send_sem=x_snd_sem.at[NY + 3 * way + hop],
            recv_sem=x_rcv_sem.at[NY + 3 * way + hop],
            device_id=at(to_z, y, core, wave),
            device_id_type=MESH,
        )
        inside = (owner >= 0) & (to_z < NZ) if way == 0 else (owner < NZ) & (to_z >= 0)
        return copy, inside

    def x_line_arrival(way, hop):
        owner = z + (-1 - hop if way == 0 else 1 + hop)
        copy = pltpu.make_async_remote_copy(
            src_ref=x_part(owner, 0, ROWS),
            dst_ref=x_part(owner, 0, ROWS),
            send_sem=x_snd_sem.at[NY + 3 * way + hop],
            recv_sem=x_rcv_sem.at[NY + 3 * way + hop],
            device_id=pal,
            device_id_type=MESH,
        )
        return copy, owner, (owner >= 0) if way == 0 else (owner < NZ)

    def x_pass(owner, owner_core):
        part = x_all.at[owner_core, pl.ds(pl.multiple_of(owner * ROWS, ROWS), ROWS)]
        return pltpu.make_async_remote_copy(
            src_ref=part,
            dst_ref=part,
            send_sem=x_fwd_sem.at[0, owner],
            recv_sem=x_fwd_sem.at[1, owner],
            device_id=pal,
            device_id_type=MESH,
        )

    def x_line_send(hop):
        for way in range(2):
            copy, inside = x_line_copy(way, hop)
            pl.when(inside)(copy.start)

    def x_line_take(hop):
        for way in range(2):
            copy, owner, present = x_line_arrival(way, hop)

            @pl.when(present)
            def _():
                copy.wait_recv()
                x_pass(owner, core).start()

    x_local = pltpu.make_async_copy(x_hbm.at[y], x_part(z, y, OWN), x_rcv_sem.at[0])
    leg_copy = pltpu.make_async_copy(leg_hbm.at[y], leg, leg_sem)

    def y_copy(kind, way, j):
        to = lax.rem(y + (1 if way == 0 else NY - 1), NY)
        return pltpu.make_async_remote_copy(
            src_ref=(snd, snd_sum)[kind].at[way, j],
            dst_ref=(rcv, rcv_sum)[kind].at[way, j],
            send_sem=snd_sem.at[kind],
            recv_sem=rcv_sem.at[kind, way, j],
            device_id=at(z, to, core, wave),
            device_id_type=MESH,
        )

    def t_copy(j):
        return pltpu.make_async_remote_copy(
            src_ref=t_snd.at[j],
            dst_ref=t_rcv.at[j],
            send_sem=t_snd_sem,
            recv_sem=t_rcv_sem.at[j],
            device_id=pal,
            device_id_type=MESH,
        )

    def z_copy(i, j):
        return pltpu.make_async_remote_copy(
            src_ref=z_snd.at[j, i],
            dst_ref=z_rcv.at[j, i],
            send_sem=z_snd_sem,
            recv_sem=z_rcv_sem.at[j],
            device_id=at(lax.rem(z + 1 + i, NZ), y, core, wave),
            device_id_type=MESH,
        )

    def shifted(z_, steps):
        return lax.rem(z_ + steps, NZ)

    block = shifted(z, NZ // 2)

    def f_copy(dy, dw):
        to_y = lax.rem(y + dy, NY)
        to_w = lax.rem(wave + dw, NW)
        return pltpu.make_async_remote_copy(
            src_ref=pieces.at[to_y, to_w],
            dst_ref=out_ref.at[y, wave],
            send_sem=f_snd_sem,
            recv_sem=f_rcv_sem,
            device_id=at(block, to_y, core, to_w),
            device_id_type=MESH,
        )

    def whole(source, target, send_sem, recv_sem):
        return pltpu.make_async_remote_copy(
            src_ref=source,
            dst_ref=target,
            send_sem=send_sem,
            recv_sem=recv_sem,
            device_id=pal,
            device_id_type=MESH,
        )

    x_pos = wave // 2
    high = lax.rem(wave, 2) * NZ + z

    def place_of(x_, y_, high_):
        return at(lax.rem(high_, NZ), y_, core, x_ * 2 + high_ // NZ)

    around = [
        place_of(lax.rem(x_pos + 1, 4), y, high),
        place_of(lax.rem(x_pos + 3, 4), y, high),
        place_of(x_pos, lax.rem(y + 1, NY), high),
        place_of(x_pos, lax.rem(y + 3, NY), high),
        place_of(x_pos, y, lax.rem(high + 1, 2 * NZ)),
        place_of(x_pos, y, lax.rem(high + 7, 2 * NZ)),
    ]

    def tell(semaphore):
        for device in around:
            pl.semaphore_signal(semaphore, inc=1, device_id=device, device_id_type=MESH)

    barrier = pltpu.get_barrier_semaphore()
    for device in (pal, at(z, lax.rem(y + 2, NY), core, wave)):
        pl.semaphore_signal(barrier, inc=1, device_id=device, device_id_type=MESH)
    tell(barrier)

    @pl.loop(0, TILES)
    def _(j):
        own_copy(j).start()

    w_local.start()
    x_local.start()
    leg_copy.start()
    pl.semaphore_wait(barrier, 2 + len(around))
    w_copy.start()

    @pl.loop(0, TILES)
    def _(j):
        for d in (2, 1, 3, 0):
            pal_copy(j, d).start()

    for dy in (2, 1, 3):
        x_copy(dy, y).start()
    tell(met.at[0])
    w_local.wait()
    w_copy.wait()
    weights = [w_ref[0:1, 0:1], w_ref[0:1, 1:2], w_pal[0:1, 0:1], w_pal[0:1, 1:2]]
    weights = [jnp.broadcast_to(v, (CHUNK, LANES)) for v in weights]

    def term_sum(j, slot, row):
        rows = pl.ds(row, CHUNK)
        r0 = raw_own[j, slot, 0, rows, :].astype(F32)
        j0 = raw_own[j, slot, 1, rows, :].astype(F32)
        r1 = raw_pal[j, slot, 0, rows, :].astype(F32)
        j1 = raw_pal[j, slot, 1, rows, :].astype(F32)
        a0, b0, a1, b1 = weights
        return (a0 * r0 - b0 * j0) + (a1 * r1 - b1 * j1), (a0 * j0 + b0 * r0) + (a1 * j1 + b1 * r1)

    def higher(height, real, imag):
        tall = jnp.maximum(jnp.abs(real), jnp.abs(imag))
        return jnp.maximum(height, jnp.max(tall.reshape(-1, 8, LANES), axis=0))

    def step_of(message, rows, size):
        step = span_of(message[rows : rows + 8, :])[0:1] * (1.0 / TOP)
        return jnp.broadcast_to(step, (size, LANES))

    def write_message(to, j, slot, halves, since):
        height = jnp.zeros((8, LANES), F32)
        for place, half in enumerate(halves):
            for part in range(QUARTER // CHUNK):
                base = part * CHUNK
                rows = slice(base, base + CHUNK)
                real, imag = term_sum(j, slot, half * QUARTER + base)
                if since is not None and place == 0:
                    more_real, more_imag = unpacked(since[rows, :], step_of(since, QUARTER, CHUNK))
                    real, imag = real + more_real, imag + more_imag
                rows = slice(place * QUARTER + base, place * QUARTER + base + CHUNK)
                work[0, rows, :] = real
                work[1, rows, :] = imag
                height = higher(height, real, imag)
        height = jnp.broadcast_to(jnp.max(height, axis=0, keepdims=True), (8, LANES))
        code = code_of(height)
        gain = jnp.broadcast_to(gain_of(code)[0:1], (CHUNK, LANES))
        total = QUARTER * len(halves)
        for part in range(total // CHUNK):
            rows = slice(part * CHUNK, (part + 1) * CHUNK)
            to[rows, :] = packed(work[0, rows, :], work[1, rows, :], gain)
        to[total : total + 8, :] = code

    def stage_first(j):
        own_copy(j).wait()
        pal_copy(j, 2).wait_recv()
        for way in range(2):
            write_message(snd.at[way, j], j, lax.rem(y + 2, NY), (way,), None)
            y_copy(0, way, j).start()

    def stage_sum(j):
        for way in range(2):
            d = 1 if way == 0 else NY - 1
            pal_copy(j, d).wait_recv()
            y_copy(0, way, j).wait_recv()
            write_message(snd_sum.at[way, j], j, lax.rem(y + d, NY), (way, 1 - way), rcv.at[way, j])
            y_copy(1, way, j).start()

    def stage_product(j):
        pal_copy(j, 0).wait_recv()
        for part in range(HALF // CHUNK):
            rows = slice(part * CHUNK, (part + 1) * CHUNK)
            work[0, rows, :], work[1, rows, :] = term_sum(j, y, part * CHUNK)
        for way in range(2):
            y_copy(1, way, j).wait_recv()
        steps = [step_of(rcv_sum.at[way, j], HALF, CHUNK) for way in range(2)]
        for half in range(2):
            for part in range(QUARTER // CHUNK):
                start = half * QUARTER + part * CHUNK
                real = work[0, start : start + CHUNK, :]
                imag = work[1, start : start + CHUNK, :]
                for way in range(2):
                    at_row = part * CHUNK + (0 if way == half else QUARTER)
                    more_real, more_imag = unpacked(
                        rcv_sum[way, j, at_row : at_row + CHUNK, :], steps[way]
                    )
                    real, imag = real + more_real, imag + more_imag
                real_high = real.astype(BF16)
                imag_high = imag.astype(BF16)
                real_low = (real - real_high.astype(F32)).astype(BF16)
                imag_low = (imag - imag_high.astype(F32)).astype(BF16)
                into = pl.ds(pl.multiple_of(core * (WINDOW - HALF) + start, CHUNK), CHUNK)
                also = pl.ds(pl.multiple_of(WINDOW + core * (WINDOW - HALF) + start, CHUNK), CHUNK)
                rhs[0, into, :] = jnp.concatenate([real_high, imag_high], axis=1)
                rhs[1, into, :] = jnp.concatenate([real_low, imag_low], axis=1)
                rhs[0, also, :] = jnp.concatenate([-imag_high, real_high], axis=1)
                rhs[1, also, :] = jnp.concatenate([-imag_low, real_low], axis=1)

        def product(owner):
            left = x_all[owner, :, pl.ds(pl.multiple_of(core * 256, LANES), WINDOW)]
            right = x_all[owner, :, pl.ds(pl.multiple_of(NDEG + core * 256, LANES), WINDOW)]
            both = jnp.concatenate([left, right], axis=1)
            value = jnp.dot(both, rhs[0], preferred_element_type=F32)
            return value + jnp.dot(both, rhs[1], preferred_element_type=F32)

        t_snd[j] = product(1 - core)
        t_copy(j).start()
        t_own[j] = product(core)

    def stage_spread(j):
        t_copy(j).wait_recv()
        own_rows = pl.ds(pl.multiple_of(block * ROWS, ROWS), ROWS)
        for turn in range(NZ - 1):
            middle = (1, 0, 2)[turn]
            i = jnp.where(z == 0, NZ - 2 - turn, jnp.where(z == NZ - 1, turn, middle))
            rows = pl.ds(pl.multiple_of(shifted(z + 1 + i, NZ // 2) * ROWS, ROWS), ROWS)
            value = t_own[j, rows, :] + t_rcv[j, rows, :]
            real, imag = value[:, :LANES], value[:, LANES:]
            height = higher(jnp.zeros((8, LANES), F32), real, imag)
            height = jnp.broadcast_to(jnp.max(height, axis=0, keepdims=True), (8, LANES))
            code = code_of(height)
            gain = jnp.broadcast_to(gain_of(code)[0:1], (ROWS, LANES))
            z_snd[j, i, :ROWS, :] = packed(real, imag, gain)
            z_snd[j, i, ROWS:, :] = code
            z_copy(i, j).start()
        t_fin[j] = t_own[j, own_rows, :] + t_rcv[j, own_rows, :]

    def stage_synthesis(j):
        whole(z_snd.at[j], z_rcv.at[j], z_snd_sem, z_rcv_sem.at[j]).wait_recv()
        value = t_fin[j]
        real, imag = value[:, :LANES], value[:, LANES:]
        for i in range(NZ - 1):
            step = span_of(z_rcv[j, i, ROWS:, :])[0:1] * (1.0 / TOP)
            step = jnp.broadcast_to(step, (ROWS, LANES))
            more_real, more_imag = unpacked(z_rcv[j, i, :ROWS, :], step)
            real, imag = real + more_real, imag + more_imag
        both = jnp.concatenate([real, imag], axis=0)
        high = both.astype(BF16)
        low = (both - high.astype(F32)).astype(BF16)
        left = jnp.concatenate([high, low], axis=1)
        table = pl.ds(pl.multiple_of(j * LANES, LANES), LANES)

        @pl.loop(0, NLAT // 256)
        def _(i):
            columns = pl.ds(pl.multiple_of(i * 256, 256), 256)
            part = leg[table, columns]
            right = jnp.concatenate([part, part], axis=0)
            grid[:, columns] += jnp.dot(left, right, preferred_element_type=F32)

    @pl.loop(0, 2)
    def _(j):
        stage_first(j)

    x_local.wait()
    for dy in range(1, NY):
        x_arrival(dy).wait_recv()
    x_line_send(0)
    x_pass(z, core).start()

    for side in range(2):
        for base in (0, WINDOW):
            pad = pl.ds(pl.multiple_of(base + (1 - core) * HALF, 64), WINDOW - HALF)
            rhs[side, pad, :] = jnp.zeros((WINDOW - HALF, 2 * LANES), BF16)
    grid[...] = jnp.zeros_like(grid)

    @pl.loop(0, TILES)
    def _(it):
        stage_sum(it)

        @pl.when(it < TILES - 2)
        def _():
            stage_first(it + 2)

        pl.semaphore_wait(met.at[it], len(around))
        tell(met.at[it + 1])

        @pl.when(it == 0)
        def _():
            x_line_take(0)
            x_line_send(1)

        @pl.when(it == 1)
        def _():
            x_line_take(1)
            x_line_send(2)

        @pl.when(it == 2)
        def _():
            x_line_take(2)
            for owner in range(NZ):
                x_pass(owner, 1 - core).wait_recv()

        @pl.when(it > 2)
        def _():
            @pl.loop(jnp.where(it == 3, 0, 2), jnp.where(it == 3, 2, 3))
            def _(j):
                stage_spread(j)

        @pl.when(it > 1)
        def _():
            @pl.loop(jnp.where(it == 2, 0, it - 1), jnp.where(it == 4, TILES, it))
            def _(j):
                stage_product(j)

                @pl.when(it == 4)
                def _():
                    stage_spread(j)

    leg_copy.wait()
    pl.semaphore_wait(met.at[MEETINGS - 1], len(around))

    @pl.loop(0, TILES)
    def _(j):
        stage_synthesis(j)

    lane = lax.broadcasted_iota(I32, (8, LANES), 1)
    @pl.loop(0, NY)
    def _(turn):
        dy = jnp.where(turn < 3, jnp.where(turn < 1, 2, turn * 2 - 1), 0)
        to_y = lax.rem(y + dy, NY)
        real = grid[pl.ds(pl.multiple_of(to_y * OWN, OWN), OWN), :]
        imag = grid[pl.ds(pl.multiple_of(ROWS + to_y * OWN, OWN), OWN), :]
        height = jnp.max(jnp.maximum(jnp.abs(real), jnp.abs(imag)), axis=1, keepdims=True)
        code = code_of(jnp.broadcast_to(height, (OWN, LANES)))
        gain = gain_of(code)
        gain = jnp.concatenate([gain] * (NLAT // LANES), axis=1)
        value = packed(real, imag, gain)
        for to_w in range(NW):
            tile, skip = divmod(to_w * BAND, LANES)
            band = value[:, tile * LANES : tile * LANES + 2 * LANES]
            if skip:
                band = pltpu.roll(band, 2 * LANES - skip, 1)
            rest = band[:, LANES:]
            last = jnp.where(lane < 96, code[:8], code[8:])
            last = jnp.where(lane < 64, pltpu.roll(rest[8:], 32, 1), last)
            last = jnp.where(lane < 32, rest[:8], last)
            pieces[to_y, to_w, :OWN, :] = band[:, :LANES]
            pieces[to_y, to_w, OWN:, :] = last

        for dw in (4, 5, 3, 2, 6, 1, 7, 0):
            f_copy(dy, dw).start()


    whole(raw_pal, raw_pal, raw_snd_sem, raw_snd_sem).wait_send()
    whole(snd, rcv, snd_sem.at[0], snd_sem.at[0]).wait_send()
    whole(snd_sum, rcv_sum, snd_sem.at[1], snd_sem.at[1]).wait_send()
    whole(t_snd, t_rcv, t_snd_sem, t_snd_sem).wait_send()
    whole(z_snd, z_rcv, z_snd_sem, z_snd_sem).wait_send()
    for d in range(1, NY):
        x_copy(d, y).wait_send()
    for hop in range(3):
        for way in range(2):
            copy, inside = x_line_copy(way, hop)
            pl.when(inside)(copy.wait_send)
    for owner in range(NZ):
        x_pass(owner, core).wait_send()

    whole(pieces, out_ref, f_snd_sem, f_rcv_sem).wait()


def exchange(spectral_state, inverse, term_weights, legendre):
    any_space = pl.BlockSpec(memory_space=pl.ANY)
    dma = pltpu.SemaphoreType.DMA
    return pl.pallas_call(
        exchange_kernel,
        out_shape=jax.ShapeDtypeStruct((NY, NW, OWN + 8, LANES), I32),
        in_specs=[any_space] * 4,
        out_specs=any_space,
        scratch_shapes=[
            pltpu.VMEM((TILES, NY, 2, HALF, LANES), BF16),
            pltpu.VMEM((TILES, NY, 2, HALF, LANES), BF16),
            pltpu.VMEM((1, 2), F32),
            pltpu.VMEM((1, 2), F32),
            pltpu.VMEM((2, NZ * NY * OWN, 2 * NDEG), BF16),
            pltpu.VMEM((NDEG, NLAT), BF16),
            pltpu.VMEM((2, TILES, QUARTER + 8, LANES), I32),
            pltpu.VMEM((2, TILES, QUARTER + 8, LANES), I32),
            pltpu.VMEM((2, TILES, HALF + 8, LANES), I32),
            pltpu.VMEM((2, TILES, HALF + 8, LANES), I32),
            pltpu.VMEM((2, HALF, LANES), F32),
            pltpu.VMEM((2, 2 * WINDOW, 2 * LANES), BF16),
            pltpu.VMEM((TILES, 256, 2 * LANES), F32),
            pltpu.VMEM((TILES, 256, 2 * LANES), F32),
            pltpu.VMEM((TILES, 256, 2 * LANES), F32),
            pltpu.VMEM((TILES, NZ - 1, ROWS + 8, LANES), I32),
            pltpu.VMEM((TILES, NZ - 1, ROWS + 8, LANES), I32),
            pltpu.VMEM((TILES, ROWS, 2 * LANES), F32),
            pltpu.VMEM((2 * ROWS, NLAT), F32),
            pltpu.VMEM((NY, NW, OWN + 8, LANES), I32),
            dma((TILES,)),
            dma,
            dma((TILES, NY)),
            dma((3,)),
            dma((NY + 6,)),
            dma((NY + 6,)),
            dma((2, NZ)),
            dma,
            dma((2,)),
            dma((2, 2, TILES)),
            dma,
            dma((TILES,)),
            dma,
            dma((TILES,)),
            dma,
            dma,
            pltpu.SemaphoreType.REGULAR((MEETINGS,)),
        ],
        compiler_params=pltpu.CompilerParams(
            collective_id=0, has_side_effects=True, vmem_limit_bytes=60 * 1024 * 1024
        ),
        name="exchange",
    )(spectral_state, inverse, term_weights, legendre)


def place_kernel(column_ref, code_ref, out_hbm, decoded, sem):
    def out_copy(slot):
        return pltpu.make_async_copy(decoded.at[slot], out_hbm.at[column_ref[slot]], sem.at[slot])

    @pl.loop(0, NW // 4)
    def _(group):
        for index in range(4 * NY):
            from_w = group * 4 + index // NY
            from_y = index % NY
            slot = from_w * NY + from_y
            last = code_ref[from_y, from_w, OWN:, :]
            moved = pltpu.roll(last, LANES - 32, 1)
            for part, rest in ((0, last), (1, moved)):
                step = span_of(rest[:, 64:65]) * (1.0 / TOP)
                main = code_ref[from_y, from_w, part * 8 : part * 8 + 8, :]
                wide = jnp.broadcast_to(step, (8, LANES))
                rows = slice(part * 8, part * 8 + 8)
                for p, value in enumerate(unpacked(main, wide)):
                    decoded[slot, p, rows, :LANES] = value
                for p, value in enumerate(unpacked(rest, wide)):
                    decoded[slot, p, rows, LANES:] = value[:, :32]
            out_copy(slot).start()

    @pl.loop(0, NW * NY)
    def _(slot):
        out_copy(slot).wait()


def place(slot_column, codes):
    shape = (NW * NY, 2, OWN, BAND)
    return pl.pallas_call(
        place_kernel,
        out_shape=jax.ShapeDtypeStruct(shape, F32),
        in_specs=[pl.BlockSpec(memory_space=pltpu.SMEM), pl.BlockSpec(memory_space=pltpu.VMEM)],
        out_specs=pl.BlockSpec(memory_space=pl.ANY),
        scratch_shapes=[pltpu.VMEM(shape, F32), pltpu.SemaphoreType.DMA((NW * NY,))],
        compiler_params=pltpu.CompilerParams(vmem_limit_bytes=60 * 1024 * 1024),
        name="place",
    )(slot_column, codes)


def shards(spectral_state, inverse, term_weights, legendre, slot_column):
    codes = exchange(spectral_state, inverse, term_weights, legendre)
    return place(slot_column, codes)


def solution(mesh):
    placed = (
        P("wave", "term", None),
        P("term", "wave", None, None, None),
        P("term", None),
        P("wave", None, None),
        P(),
    )
    return jax.shard_map(
        shards, mesh=mesh, in_specs=placed, out_specs=P(None, None, "term", "wave"), check_vma=False
    )
```
